256 devices in a mesh: ctx: 32 (over y, z_hi, x), tp: 8 (over z_lo, core).
Axes of the slice: x: 4, y: 4, z: 8 (z_hi: 2, z_lo: 4; z = z_hi * 4 + z_lo), core: 2. Of those that a mesh axis runs over, the one named last changes fastest.
Arguments:
- query_feats: bfloat16 [8192, 8192], P('ctx', 'tp'), may hold values from -6 to 6
- key_feats: bfloat16 [8192, 8192], P('ctx', 'tp'), may hold values from -6 to 6
- value_feats: bfloat16 [8192, 8192], P('ctx', 'tp'), may hold values from -6 to 6
- short_taps: float32 [3, 7, 512], P(None, None, 'tp'), may hold values from -2 to 2
- long_filter: bfloat16 [8192, 512], P('ctx', 'tp'), may hold values from -6 to 6
- skip_gain: float32 [8192], P('tp'), may hold values from -1 to 1
- out_grad: bfloat16 [8192, 8192], P('ctx', 'tp'), may hold values from -6 to 6
Outputs:
- mixed_out: bfloat16 [8192, 8192], P('ctx', 'tp')
- grad_query: bfloat16 [8192, 8192], P('ctx', 'tp')
- grad_key: bfloat16 [8192, 8192], P('ctx', 'tp')
- grad_value: bfloat16 [8192, 8192], P('ctx', 'tp')
- grad_filter: bfloat16 [8192, 512], P('ctx', 'tp')
The draws below stay inside these ranges and needn't reach their ends.
All inputs are finite; a program needn't handle non-finite values.
Results may differ from the reference program's by a relative error of at most 0.0058.
Values may be sent and summed in bfloat16 or wider, within the bound.
No kernel may reach another device: no remote copies, remote signals or barrier semaphores. Data moves between devices by JAX's collectives and lax.ppermute only.
A program may use at most 128 MiB of HBM per device.

```python
import math
import jax
import jax.numpy as jnp
from jax import lax

D = 8192
SHORT_GROUPS = 512
TAPS = 7
SEQ = 8192


def block_scale(stream_key, shape, split, smallest, top_value):
    level = 1.0
    for axis_at, shards_of in split:
        draws = jax.random.uniform(jax.random.fold_in(jax.random.fold_in(stream_key, 6), axis_at), (shards_of,), jnp.float32, smallest / len(split), top_value / len(split))
        level = level * jnp.repeat(jnp.exp(draws), shape[axis_at] // shards_of).reshape((-1,) + (1,) * (len(shape) - 1 - axis_at))
    return level


def bell_draw(stream_key, dims, scale, bound, cuts=(), kind=jnp.bfloat16):
    drawn = scale * jax.random.normal(stream_key, dims, jnp.float32)
    if cuts:
        drawn = drawn * block_scale(stream_key, dims, cuts, -0.22, 0.18)
    return jnp.clip(drawn, -bound, bound).astype(kind)


def setup_inputs(seed: int = 0) -> dict:
    arg_keys = jax.random.split(jax.random.key(seed), 8)
    return {
        "query_feats": bell_draw(arg_keys[0], (SEQ, D), 1.0, 6.0, ((0, 32), (1, 8))),
        "key_feats": bell_draw(arg_keys[1], (SEQ, D), 1.0, 6.0, ((0, 32), (1, 8))),
        "value_feats": bell_draw(arg_keys[2], (SEQ, D), 1.0, 6.0, ((0, 32), (1, 8))),
        "short_taps": bell_draw(arg_keys[3], (3, TAPS, SHORT_GROUPS), TAPS ** -0.5, 2.0, ((2, 8),), jnp.float32),
        "long_filter": bell_draw(arg_keys[4], (SEQ, SHORT_GROUPS), 1.0, 6.0, ((0, 32), (1, 8))),
        "skip_gain": jnp.clip(jax.random.uniform(arg_keys[5], (D,), jnp.float32, -1.0, 1.0) * block_scale(arg_keys[5], (D,), ((0, 8),), -0.4, 0.0), -1.0, 1.0),
        "out_grad": bell_draw(arg_keys[6], (SEQ, D), 1.0, 6.0, ((0, 32), (1, 8))),
    }


def causal_sum(signal, taps):
    count = taps.shape[0]
    length = signal.shape[0]
    padded = jnp.pad(signal, ((count - 1, 0), (0, 0)))
    total = jnp.zeros_like(signal)
    for offset in range(count):
        total = total + taps[offset] * padded[count - 1 - offset:count - 1 - offset + length]
    return total


def anti_sum(signal, taps):
    count = taps.shape[0]
    length = signal.shape[0]
    padded = jnp.pad(signal, ((0, count - 1), (0, 0)))
    total = jnp.zeros_like(signal)
    for offset in range(count):
        total = total + taps[offset] * padded[offset:offset + length]
    return total


def block_pass(pieces):
    queries, keys_in, values_in, taps, filt_raw, skip, grad_out = pieces
    scale = SEQ ** -0.5
    size = 2 * SEQ
    group = D // SHORT_GROUPS
    query_conv = causal_sum(queries.astype(jnp.float32), taps[0])
    key_conv = causal_sum(keys_in.astype(jnp.float32), taps[1])
    value_conv = causal_sum(values_in.astype(jnp.float32), taps[2])
    gated = (key_conv * value_conv).astype(jnp.bfloat16)
    gated_full = gated.astype(jnp.float32)
    group_spec = jnp.fft.rfft(filt_raw.astype(jnp.float32) * scale, n=size, axis=0)
    filt_spec = jnp.repeat(group_spec, group, axis=1)
    gated_spec = jnp.fft.rfft(gated_full, n=size, axis=0)
    conv = jnp.fft.irfft(gated_spec * filt_spec, n=size, axis=0)[:SEQ].astype(jnp.bfloat16)
    mixed = conv.astype(jnp.float32) + skip * gated_full
    output = (query_conv * mixed).astype(jnp.bfloat16)
    grad_full = grad_out.astype(jnp.float32)
    grad_mix = (grad_full * query_conv).astype(jnp.bfloat16)
    grad_mix_full = grad_mix.astype(jnp.float32)
    grad_spec = jnp.fft.rfft(grad_mix_full, n=size, axis=0)
    back_conv = jnp.fft.irfft(grad_spec * jnp.conj(filt_spec), n=size, axis=0)[:SEQ].astype(jnp.bfloat16)
    cross = grad_spec * jnp.conj(gated_spec)
    cross = cross.reshape(cross.shape[0], -1, group).sum(axis=2)
    filt_grad = (jnp.fft.irfft(cross, n=size, axis=0)[:SEQ] * scale).astype(jnp.bfloat16)
    grad_gate = back_conv.astype(jnp.float32) + skip * grad_mix_full
    grad_qconv = grad_full * mixed
    grad_kconv = grad_gate * value_conv
    grad_vconv = grad_gate * key_conv
    grad_q = anti_sum(grad_qconv, taps[0]).astype(jnp.bfloat16)
    grad_k = anti_sum(grad_kconv, taps[1]).astype(jnp.bfloat16)
    grad_v = anti_sum(grad_vconv, taps[2]).astype(jnp.bfloat16)
    return (output, grad_q, grad_k, grad_v, filt_grad)


def reference(query_feats, key_feats, value_feats, short_taps, long_filter, skip_gain, out_grad):
    block = math.gcd(D, 512)
    count = D // block
    group = D // SHORT_GROUPS
    gblock = block // group

    def split_cols(array):
        return array.reshape(SEQ, count, block).transpose(1, 0, 2)

    def join_cols(array):
        return array.transpose(1, 0, 2).reshape(SEQ, D)

    taps_full = jnp.repeat(short_taps.astype(jnp.float32), group, axis=2)
    taps_blocks = taps_full.reshape(3, TAPS, count, block).transpose(2, 0, 1, 3)
    skips = skip_gain.astype(jnp.float32).reshape(count, block)
    filt_blocks = long_filter.reshape(SEQ, count, gblock).transpose(1, 0, 2)
    results = lax.map(block_pass, (split_cols(query_feats), split_cols(key_feats), split_cols(value_feats), taps_blocks, filt_blocks, skips, split_cols(out_grad)))
    filt_grad = results[4].transpose(1, 0, 2).reshape(SEQ, SHORT_GROUPS)
    return (join_cols(results[0]), join_cols(results[1]), join_cols(results[2]), join_cols(results[3]), filt_grad)
```

```python
import functools
import math

import jax
import jax.numpy as jnp
from jax import lax
from jax.experimental import pallas as pl
from jax.experimental.pallas import tpu as pltpu
from jax.sharding import PartitionSpec as P

D = 8192
SHORT_GROUPS = 512
GROUP = D // SHORT_GROUPS
TAPS = 7
HALO = 8
LANES = 128
VMEM_LIMIT = 50 * 1024 * 1024

f32 = jnp.float32
bf16 = jnp.bfloat16


def shifted(value, axis, steps):
    count = lax.axis_size(axis)
    initial, last = (max(0, -steps), min(count, count - steps))
    return lax.ppermute(value, axis, [(source, source + steps) for source in range(initial, last)])


def featurize_kernel(q_ref, k_ref, v_ref, g_ref, before_ref, taps_ref, x_ref, qc_ref, kc_ref, vc_ref, ext):
    rows, cols = q_ref.shape

    def conv(which, ref):
        ext[:HALO, :] = before_ref[which].astype(f32)
        ext[HALO:, :] = ref[...].astype(f32)
        total = taps_ref[which, 0:1, :] * ext[HALO : HALO + rows, :]
        for offset in range(1, TAPS):
            total = total + taps_ref[which, offset : offset + 1, :] * ext[HALO - offset : HALO - offset + rows, :]
        return total

    def emit(value, lo):
        owners = x_ref.shape[0]
        x_ref[:, lo : lo + cols // owners, :] = value.T.astype(bf16).reshape(owners, cols // owners, rows)

    half = x_ref.shape[1] // 2
    key_conv = conv(1, k_ref)
    kc_ref[...] = key_conv
    value_conv = conv(2, v_ref)
    vc_ref[...] = value_conv
    emit(key_conv * value_conv, 0)
    query_conv = conv(0, q_ref)
    qc_ref[...] = query_conv
    emit(g_ref[...].astype(f32) * query_conv, half)


def featurize(query, key, value, grad, before, taps_full, n_ctx):
    rows, width = query.shape
    owned = width // n_ctx
    cols = LANES
    steps = width // cols
    tok = pl.BlockSpec((rows, cols), lambda i: (0, i))
    return pl.pallas_call(
        featurize_kernel,
        grid=(steps,),
        in_specs=[
            tok,
            tok,
            tok,
            tok,
            pl.BlockSpec((3, HALO, cols), lambda i: (0, 0, i)),
            pl.BlockSpec((3, TAPS, cols), lambda i: (0, 0, i)),
        ],
        out_specs=[
            pl.BlockSpec((cols // owned, 2 * owned, rows), lambda i: (i, 0, 0)),
            tok,
            tok,
            tok,
        ],
        out_shape=[
            jax.ShapeDtypeStruct((n_ctx, 2 * owned, rows), bf16),
            jax.ShapeDtypeStruct((rows, width), f32),
            jax.ShapeDtypeStruct((rows, width), f32),
            jax.ShapeDtypeStruct((rows, width), f32),
        ],
        scratch_shapes=[pltpu.VMEM((rows + HALO, cols), f32)],
        compiler_params=pltpu.CompilerParams(vmem_limit_bytes=VMEM_LIMIT),
        name="featurize",
    )(query, key, value, grad, before, taps_full)


WIDE = 2048


def shift_right(value, steps):
    return value if steps == 0 else pltpu.roll(value, steps, axis=1)


def shift_left(value, steps):
    return value if steps == 0 else pltpu.roll(value, value.shape[1] - steps, axis=1)


def build_toeplitz(f_ref, fpad, v8, toe):
    length = f_ref.shape[-1]
    fpad[:, :LANES] = jnp.zeros((1, LANES), f32)
    fpad[:, LANES : 2 * LANES] = jnp.zeros((1, LANES), f32)
    fpad[:, 2 * LANES :] = f_ref[0].astype(f32)
    for lo in range(0, length, WIDE):
        wide = jnp.broadcast_to(fpad[:, lo + LANES : lo + 2 * LANES + WIDE], (8, WIDE + LANES))
        row = lax.broadcasted_iota(jnp.int32, wide.shape, 0)
        for bit in (1, 2, 4):
            wide = jnp.where((row & bit) != 0, shift_right(wide, bit), wide)
        v8[:, lo + LANES : lo + LANES + WIDE] = wide[:, LANES:]
    v8[:, :LANES] = jnp.zeros((8, LANES), f32)
    toe[:, :LANES] = jnp.zeros((LANES, LANES), bf16)

    for lo in range(0, length, WIDE):
        wide = v8[:, lo : lo + LANES + WIDE]
        for p in range(0, LANES // 8, 2):
            pair = [shift_right(wide, 8 * (p + i))[:, LANES:] for i in range(2)]
            toe[8 * p : 8 * p + 16, lo + LANES : lo + LANES + WIDE] = jnp.concatenate(pair, axis=0).astype(bf16)


def longconv_kernel(x_ref, f_ref, y_ref, fg_ref, fpad, v8, toe, gpad, zpad, acc, corr, *, scale):
    blocks, _, _, group, size = x_ref.shape
    length = blocks * size
    rows = blocks * group
    batch = 4
    top = batch * group
    build_toeplitz(f_ref, fpad, v8, toe)
    gpad[:top, :] = jnp.zeros((top, size), bf16)
    gpad[top:, :] = x_ref[:, 0, 0].reshape(rows, size)
    zpad[:rows, :] = x_ref[:, 1, 0].reshape(rows, size)
    zpad[rows:, :] = jnp.zeros((zpad.shape[0] - rows, size), bf16)

    u_t = gpad[top:, :].astype(f32).T.astype(bf16)
    half = rows // 2
    for k in range(blocks):
        depth = rows if k < blocks // 2 else half
        corr[:, size * k : size * (k + 1)] = jnp.dot(
            u_t[:, :depth], zpad[group * k : group * k + depth, :], preferred_element_type=f32
        )
    corr[:, length:] = jnp.zeros((size, corr.shape[1] - length), f32)
    for lo in range(0, length, WIDE):
        total = None
        for p in reversed(range(LANES // 8)):
            part = (
                corr[8 * p : 8 * p + 8, lo : lo + WIDE + LANES]
                + corr[LANES + 8 * p : LANES + 8 * p + 8, lo + LANES : lo + WIDE + 2 * LANES]
            )
            total = part if total is None else shift_left(total, 8) + part
        row = lax.broadcasted_iota(jnp.int32, total.shape, 0)
        for bit in (4, 2, 1):
            total = jnp.where((row & bit) != 0, shift_left(total, bit), total)
        fg_ref[0, :, lo : lo + WIDE] = (jnp.sum(total[:, :WIDE], axis=0, keepdims=True) * scale).astype(bf16)

    def toeplitz_rows(k, width):
        base = 2 * k * LANES
        return jnp.concatenate(
            [toe[:, base + LANES : base + LANES + width], toe[:, base : base + width]], axis=0
        )

    left = jnp.concatenate([gpad[top - group * i : top - group * i + rows, :] for i in range(batch)], axis=1)
    for kb in range(blocks // batch):
        first = top * kb
        right = jnp.concatenate([toeplitz_rows(batch * kb + i, size) for i in range(batch)], axis=0)
        part = jnp.dot(left[: rows - first], right, preferred_element_type=f32)
        acc[first:, :] = part if kb == 0 else acc[first:, :] + part
    y_ref[:, 0, 0] = (acc[...] * scale).astype(bf16).reshape(blocks, group, size)

    for kb in range(blocks // batch):
        first = top * kb
        right = toeplitz_rows(batch * kb, batch * size)
        count = rows - first
        left = jnp.concatenate(
            [zpad[first + group * i : first + group * i + count, :] for i in range(batch)], axis=1
        )
        part = lax.dot_general(left, right, (((1,), (1,)), ((), ())), preferred_element_type=f32)
        acc[:count, :] = part if kb == 0 else acc[:count, :] + part
    y_ref[:, 1, 0] = (acc[...] * scale).astype(bf16).reshape(blocks, group, size)


def longconv(x, filt, scale):
    blocks, both, size = x.shape
    groups = filt.shape[0]
    length = blocks * size
    rows = blocks * GROUP
    x5 = x.reshape(blocks, 2, groups, GROUP, size)
    block5 = pl.BlockSpec((blocks, 2, 1, GROUP, size), lambda g: (0, 0, g, 0, 0))
    lag = pl.BlockSpec((1, 1, length), lambda g: (g, 0, 0))
    y5, fgrad = pl.pallas_call(
        functools.partial(longconv_kernel, scale=scale),
        grid=(groups,),
        in_specs=[block5, lag],
        out_specs=[block5, lag],
        out_shape=[
            jax.ShapeDtypeStruct(x5.shape, bf16),
            jax.ShapeDtypeStruct((groups, 1, length), bf16),
        ],
        scratch_shapes=[
            pltpu.VMEM((1, length + 2 * LANES), f32),
            pltpu.VMEM((8, length + LANES), f32),
            pltpu.VMEM((LANES, length + LANES), bf16),
            pltpu.VMEM((rows + 4 * GROUP, size), bf16),
            pltpu.VMEM((rows + rows // 2, size), bf16),
            pltpu.VMEM((rows, size), f32),
            pltpu.VMEM((size, length + 2 * LANES), f32),
        ],
        compiler_params=pltpu.CompilerParams(vmem_limit_bytes=VMEM_LIMIT),
        name="longconv",
    )(x5, filt.reshape(groups, 1, length))
    return y5.reshape(x.shape), fgrad.reshape(groups, length)


def tokens(y_ref, lo, count, lanes):
    owners = y_ref.shape[0]
    return y_ref[:, lo : lo + count, :lanes].astype(f32).reshape(owners * count, lanes).T


def grads(conv, back, qc, kc, vc, grad, skip):
    gated = (kc * vc).astype(bf16).astype(f32)
    grad_mix = (grad * qc).astype(bf16).astype(f32)
    mixed = conv + skip * gated
    grad_gate = back + skip * grad_mix
    return mixed, grad * mixed, grad_gate * vc, grad_gate * kc


def heads_kernel(y_ref, qc_ref, kc_ref, vc_ref, g_ref, skip_ref, out_ref):
    half = y_ref.shape[1] // 2
    conv = tokens(y_ref, 0, half, LANES)[:HALO]
    back = tokens(y_ref, half, half, LANES)[:HALO]
    grad = g_ref[...].astype(f32)[:HALO]
    _, gq, gk, gv = grads(conv, back, qc_ref[...], kc_ref[...], vc_ref[...], grad, skip_ref[...])
    out_ref[0] = gq.astype(bf16)
    out_ref[1] = gk.astype(bf16)
    out_ref[2] = gv.astype(bf16)


def heads(y, qc, kc, vc, grad, skip):
    n_ctx, both, rows = y.shape
    width = qc.shape[1]
    cols = 512
    top = pl.BlockSpec((HALO, cols), lambda i: (0, i))
    return pl.pallas_call(
        heads_kernel,
        grid=(width // cols,),
        in_specs=[
            pl.BlockSpec((cols // (both // 2), both, LANES), lambda i: (i, 0, 0)),
            top,
            top,
            top,
            pl.BlockSpec((2 * HALO, cols), lambda i: (0, i)),
            pl.BlockSpec((1, cols), lambda i: (0, i)),
        ],
        out_specs=pl.BlockSpec((3, HALO, cols), lambda i: (0, 0, i)),
        out_shape=jax.ShapeDtypeStruct((3, HALO, width), bf16),
        compiler_params=pltpu.CompilerParams(vmem_limit_bytes=VMEM_LIMIT),
        name="heads",
    )(y, qc, kc, vc, grad, skip)


def spread_kernel(
    y_ref, qc_ref, kc_ref, vc_ref, g_ref, skip_ref, after_ref, taps_ref, out_ref, gq_ref, gk_ref, gv_ref, ext
):
    rows = qc_ref.shape[0]
    half = y_ref.shape[1] // 2
    conv = tokens(y_ref, 0, half, rows)
    back = tokens(y_ref, half, half, rows)
    query_conv = qc_ref[...]
    mixed, gq, gk, gv = grads(
        conv, back, query_conv, kc_ref[...], vc_ref[...], g_ref[...].astype(f32), skip_ref[...]
    )
    out_ref[...] = (query_conv * mixed).astype(bf16)
    for which, (signal, target) in enumerate(((gq, gq_ref), (gk, gk_ref), (gv, gv_ref))):
        ext[:rows, :] = signal
        ext[rows:, :] = after_ref[which].astype(f32)
        total = taps_ref[which, 0:1, :] * ext[:rows, :]
        for offset in range(1, TAPS):
            total = total + taps_ref[which, offset : offset + 1, :] * ext[offset : offset + rows, :]
        target[...] = total.astype(bf16)


def spread(y, qc, kc, vc, grad, skip, after, taps_full):
    n_ctx, both, rows = y.shape
    width = qc.shape[1]
    cols = LANES
    tok = pl.BlockSpec((rows, cols), lambda i: (0, i))
    return pl.pallas_call(
        spread_kernel,
        grid=(width // cols,),
        in_specs=[
            pl.BlockSpec((cols // (both // 2), both, rows), lambda i: (i, 0, 0)),
            tok,
            tok,
            tok,
            tok,
            pl.BlockSpec((1, cols), lambda i: (0, i)),
            pl.BlockSpec((3, HALO, cols), lambda i: (0, 0, i)),
            pl.BlockSpec((3, TAPS, cols), lambda i: (0, 0, i)),
        ],
        out_specs=[tok] * 4,
        out_shape=[jax.ShapeDtypeStruct((rows, width), bf16)] * 4,
        scratch_shapes=[pltpu.VMEM((rows + HALO, cols), f32)],
        compiler_params=pltpu.CompilerParams(vmem_limit_bytes=VMEM_LIMIT),
        name="spread",
    )(y, qc, kc, vc, grad, skip, after, taps_full)


def body(query_feats, key_feats, value_feats, short_taps, long_filter, skip_gain, out_grad):
    tok_rows, width = query_feats.shape
    group_cols = long_filter.shape[1]
    n_ctx = lax.axis_size("ctx")
    me = lax.axis_index("ctx")
    owned_groups = group_cols // n_ctx
    length = tok_rows * n_ctx
    taps_full = jnp.repeat(short_taps, GROUP, axis=2)
    skip = skip_gain.reshape(1, width)
    rims = jnp.stack([a[tok_rows - HALO :] for a in (query_feats, key_feats, value_feats)])
    before = shifted(rims, "ctx", 1)
    filt_all = lax.all_gather(long_filter.T, "ctx", axis=0, tiled=False)
    filt = lax.dynamic_slice_in_dim(filt_all, me * owned_groups, owned_groups, 1)
    filt = filt.transpose(1, 0, 2).reshape(owned_groups, length)
    x, qc, kc, vc = featurize(query_feats, key_feats, value_feats, out_grad, before, taps_full, n_ctx)
    x = lax.all_to_all(x, "ctx", 0, 0, tiled=True)
    y, fgrad = longconv(x, filt, 1.0 / math.sqrt(length))
    fgrad_all = lax.all_gather(fgrad, "ctx", axis=0, tiled=True)
    grad_filter = lax.dynamic_slice_in_dim(fgrad_all, me * tok_rows, tok_rows, 1).T
    y = lax.all_to_all(y, "ctx", 0, 0, tiled=True)
    after = shifted(heads(y, qc, kc, vc, out_grad, skip), "ctx", -1)
    mixed_out, gq, gk, gv = spread(y, qc, kc, vc, out_grad, skip, after, taps_full)
    return (mixed_out, gq, gk, gv, grad_filter)


def solution(mesh):
    in_specs = (
        P("ctx", "tp"),
        P("ctx", "tp"),
        P("ctx", "tp"),
        P(None, None, "tp"),
        P("ctx", "tp"),
        P("tp"),
        P("ctx", "tp"),
    )
    out_specs = (P("ctx", "tp"),) * 5
    return jax.shard_map(body, mesh=mesh, in_specs=in_specs, out_specs=out_specs, check_vma=False)
```

```python
import functools
import math

import jax
import jax.numpy as jnp
from jax import lax
from jax.experimental import pallas as pl
from jax.experimental.pallas import tpu as pltpu
from jax.sharding import PartitionSpec as P

D = 8192
SHORT_GROUPS = 512
GROUP = D // SHORT_GROUPS
TAPS = 7
HALO = 8
TAIL = 16
SPARE = 8
LANES = 128
VMEM_LIMIT = 30 * 1024 * 1024

f32 = jnp.float32
bf16 = jnp.bfloat16


def shifted(value, axis, steps):
    count = lax.axis_size(axis)
    initial, last = (max(0, -steps), min(count, count - steps))
    return lax.ppermute(value, axis, [(source, source + steps) for source in range(initial, last)])


def featurize_kernel(q_ref, k_ref, v_ref, g_ref, before_ref, taps_ref, f_ref, x_ref, qc_ref, kc_ref, vc_ref, ext):
    rows, cols = q_ref.shape
    owners = x_ref.shape[0]
    half = cols // owners
    owned_groups = f_ref.shape[0] // owners

    def conv(which, ref):
        ext[:HALO, :] = before_ref[which].astype(f32)
        ext[HALO:, :] = ref[...].astype(f32)
        total = taps_ref[which, 0:1, :] * ext[HALO : HALO + rows, :]
        for offset in range(1, TAPS):
            total = total + taps_ref[which, offset : offset + 1, :] * ext[HALO - offset : HALO - offset + rows, :]
        return total

    def emit(value, lo):
        x_ref[:, lo : lo + half, :] = value.T.astype(bf16).reshape(owners, half, rows)

    filt = f_ref[...].astype(f32)
    blank = jnp.zeros((SPARE - owned_groups, rows), f32)
    for owner in range(owners):
        lines = filt[owner * owned_groups : (owner + 1) * owned_groups]
        x_ref[owner, 2 * half :, :] = jnp.concatenate([lines, blank], axis=0).astype(bf16)
    key_conv = conv(1, k_ref)
    kc_ref[...] = key_conv
    value_conv = conv(2, v_ref)
    vc_ref[...] = value_conv
    emit(key_conv * value_conv, 0)
    query_conv = conv(0, q_ref)
    qc_ref[...] = query_conv
    emit(g_ref[...].astype(f32) * query_conv, half)


def in_hbm(*arrays):
    return [pltpu.with_memory_space_constraint(a, pltpu.HBM) for a in arrays]


def featurize(query, key, value, grad, before, taps_full, filt, n_ctx):
    rows, width = query.shape
    chunk = 2 * (width // n_ctx) + SPARE
    owned = width // n_ctx
    cols = LANES
    steps = width // cols
    tok = pl.BlockSpec((rows, cols), lambda i: (0, i))
    return pl.pallas_call(
        featurize_kernel,
        grid=(steps,),
        in_specs=[
            tok,
            tok,
            tok,
            tok,
            pl.BlockSpec((3, HALO, cols), lambda i: (0, 0, i)),
            pl.BlockSpec((3, TAPS, cols), lambda i: (0, 0, i)),
            pl.BlockSpec((cols // GROUP, rows), lambda i: (i, 0)),
        ],
        out_specs=[
            pl.BlockSpec((cols // owned, chunk, rows), lambda i: (i, 0, 0)),
            tok,
            tok,
            tok,
        ],
        out_shape=[
            pltpu.HBM((n_ctx, chunk, rows), bf16),
            jax.ShapeDtypeStruct((rows, width), f32),
            jax.ShapeDtypeStruct((rows, width), f32),
            jax.ShapeDtypeStruct((rows, width), f32),
        ],
        scratch_shapes=[pltpu.VMEM((rows + HALO, cols), f32)],
        compiler_params=pltpu.CompilerParams(vmem_limit_bytes=VMEM_LIMIT),
        name="featurize",
    )(*in_hbm(query, key, value, grad), before, taps_full, filt)


WIDE = 2048


def shift_right(value, steps):
    return value if steps == 0 else pltpu.roll(value, steps, axis=1)


def shift_left(value, steps):
    return value if steps == 0 else pltpu.roll(value, value.shape[1] - steps, axis=1)


def build_toeplitz(fpad, which, length, v8, toe):
    for lo in range(0, length, WIDE):
        wide = jnp.broadcast_to(fpad[pl.ds(which, 1), lo + LANES : lo + 2 * LANES + WIDE], (8, WIDE + LANES))
        row = lax.broadcasted_iota(jnp.int32, wide.shape, 0)
        for bit in (1, 2, 4):
            wide = jnp.where((row & bit) != 0, shift_right(wide, bit), wide)
        v8[:, lo + LANES : lo + LANES + WIDE] = wide[:, LANES:]
    v8[:, :LANES] = jnp.zeros((8, LANES), f32)
    toe[:, :LANES] = jnp.zeros((LANES, LANES), bf16)

    for lo in range(0, length, WIDE):
        wide = v8[:, lo : lo + LANES + WIDE]
        for p in range(0, LANES // 8, 2):
            pair = [shift_right(wide, 8 * (p + i))[:, LANES:] for i in range(2)]
            toe[8 * p : 8 * p + 16, lo + LANES : lo + LANES + WIDE] = jnp.concatenate(pair, axis=0).astype(bf16)


def longconv_kernel(x_ref, y_hbm, fpad, v8, toe, gpad, zpad, acc, corr, fgrad, y_ref, sems, *, scale):
    g = pl.program_id(0)
    blocks, chunk, size = x_ref.shape
    half = (chunk - SPARE) // 2
    length = blocks * size
    rows = blocks * GROUP
    group = GROUP
    batch = 4
    top = batch * group

    @pl.when(g == 0)
    def _():
        fpad[:, : 2 * LANES] = jnp.zeros((SPARE, 2 * LANES), f32)
        for j in range(blocks):
            lo = 2 * LANES + size * j
            fpad[:, lo : lo + size] = x_ref[j, 2 * half :, :].astype(f32)
        fgrad[...] = jnp.zeros_like(fgrad)

    build_toeplitz(fpad, g, length, v8, toe)
    gpad[:top, :] = jnp.zeros((top, size), bf16)
    lines = pl.ds(pl.multiple_of(g * group, group), group)
    back_lines = pl.ds(pl.multiple_of(half + g * group, group), group)
    gpad[top:, :] = x_ref[:, lines, :].reshape(rows, size)
    zpad[:rows, :] = x_ref[:, back_lines, :].reshape(rows, size)
    zpad[rows:, :] = jnp.zeros((zpad.shape[0] - rows, size), bf16)

    u_t = gpad[top:, :].astype(f32).T.astype(bf16)
    near = rows // 2
    for k in range(blocks):
        depth = rows if k < blocks // 2 else near
        corr[:, size * k : size * (k + 1)] = jnp.dot(
            u_t[:, :depth], zpad[group * k : group * k + depth, :], preferred_element_type=f32
        )
    corr[:, length:] = jnp.zeros((size, corr.shape[1] - length), f32)
    for lo in range(0, length, WIDE):
        total = None
        for p in reversed(range(LANES // 8)):
            part = (
                corr[8 * p : 8 * p + 8, lo : lo + WIDE + LANES]
                + corr[LANES + 8 * p : LANES + 8 * p + 8, lo + LANES : lo + WIDE + 2 * LANES]
            )
            total = part if total is None else shift_left(total, 8) + part
        row = lax.broadcasted_iota(jnp.int32, total.shape, 0)
        for bit in (4, 2, 1):
            total = jnp.where((row & bit) != 0, shift_left(total, bit), total)
        fgrad[pl.ds(g, 1), lo : lo + WIDE] = jnp.sum(total[:, :WIDE], axis=0, keepdims=True) * scale

    def toeplitz_rows(k, width):
        base = 2 * k * LANES
        return jnp.concatenate(
            [toe[:, base + LANES : base + LANES + width], toe[:, base : base + width]], axis=0
        )

    left = jnp.concatenate([gpad[top - group * i : top - group * i + rows, :] for i in range(batch)], axis=1)
    for kb in range(blocks // batch):
        first = top * kb
        right = jnp.concatenate([toeplitz_rows(batch * kb + i, size) for i in range(batch)], axis=0)
        part = jnp.dot(left[: rows - first], right, preferred_element_type=f32)
        acc[first:, :] = part if kb == 0 else acc[first:, :] + part
    y_ref[:, lines, :] = (acc[...] * scale).astype(bf16).reshape(blocks, group, size)
    conv_out = pltpu.make_async_copy(y_ref.at[:, lines, :], y_hbm.at[:, lines, :], sems.at[0])
    conv_out.start()

    for kb in range(blocks // batch):
        first = top * kb
        right = toeplitz_rows(batch * kb, batch * size)
        count = rows - first
        left = jnp.concatenate(
            [zpad[first + group * i : first + group * i + count, :] for i in range(batch)], axis=1
        )
        part = lax.dot_general(left, right, (((1,), (1,)), ((), ())), preferred_element_type=f32)
        acc[:count, :] = part if kb == 0 else acc[:count, :] + part
    y_ref[:, back_lines, :] = (acc[...] * scale).astype(bf16).reshape(blocks, group, size)
    back_out = pltpu.make_async_copy(y_ref.at[:, back_lines, :], y_hbm.at[:, back_lines, :], sems.at[1])
    back_out.start()

    @pl.when(g == pl.num_programs(0) - 1)
    def _():
        for j in range(blocks):
            y_ref[j, 2 * half :, :] = fgrad[:, size * j : size * (j + 1)].astype(bf16)
        spare = pl.ds(2 * half, SPARE)
        spare_out = pltpu.make_async_copy(y_ref.at[:, spare, :], y_hbm.at[:, spare, :], sems.at[2])
        spare_out.start()
        spare_out.wait()

    conv_out.wait()
    back_out.wait()


def longconv(x, scale):
    blocks, chunk, size = x.shape
    length = blocks * size
    rows = blocks * GROUP
    groups = (chunk - SPARE) // 2 // GROUP
    return pl.pallas_call(
        functools.partial(longconv_kernel, scale=scale),
        grid=(groups,),
        in_specs=[pl.BlockSpec(memory_space=pltpu.VMEM)],
        out_specs=pl.BlockSpec(memory_space=pltpu.HBM),
        out_shape=pltpu.HBM(x.shape, bf16),
        scratch_shapes=[
            pltpu.VMEM((SPARE, length + 2 * LANES), f32),
            pltpu.VMEM((8, length + LANES), f32),
            pltpu.VMEM((LANES, length + LANES), bf16),
            pltpu.VMEM((rows + 4 * GROUP, size), bf16),
            pltpu.VMEM((rows + rows // 2, size), bf16),
            pltpu.VMEM((rows, size), f32),
            pltpu.VMEM((size, length + 2 * LANES), f32),
            pltpu.VMEM((SPARE, length), f32),
            pltpu.VMEM(x.shape, bf16),
            pltpu.SemaphoreType.DMA((3,)),
        ],
        compiler_params=pltpu.CompilerParams(vmem_limit_bytes=VMEM_LIMIT),
        name="longconv",
    )(x)


def tokens(y_ref, lo, count, lanes):
    owners = y_ref.shape[0]
    return y_ref[:, lo : lo + count, :lanes].astype(f32).reshape(owners * count, lanes).T


def grads(conv, back, qc, kc, vc, grad, skip):
    gated = (kc * vc).astype(bf16).astype(f32)
    grad_mix = (grad * qc).astype(bf16).astype(f32)
    mixed = conv + skip * gated
    grad_gate = back + skip * grad_mix
    return mixed, grad * mixed, grad_gate * vc, grad_gate * kc


def anti_sum(taps_ref, which, ext, count):
    total = taps_ref[which, 0:1, :] * ext[:count, :]
    for offset in range(1, TAPS):
        total = total + taps_ref[which, offset : offset + 1, :] * ext[offset : offset + count, :]
    return total


def heads_kernel(y_ref, qc_ref, kc_ref, vc_ref, g_ref, skip_ref, out_ref):
    half = (y_ref.shape[1] - SPARE) // 2
    conv = tokens(y_ref, 0, half, LANES)[:HALO]
    back = tokens(y_ref, half, half, LANES)[:HALO]
    grad = g_ref[...].astype(f32)[:HALO]
    _, gq, gk, gv = grads(conv, back, qc_ref[...], kc_ref[...], vc_ref[...], grad, skip_ref[...])
    out_ref[0] = gq.astype(bf16)
    out_ref[1] = gk.astype(bf16)
    out_ref[2] = gv.astype(bf16)


def heads(y, qc, kc, vc, grad, skip):
    n_ctx, chunk, rows = y.shape
    width = qc.shape[1]
    cols = 512
    top = pl.BlockSpec((HALO, cols), lambda i: (0, i))
    return pl.pallas_call(
        heads_kernel,
        grid=(width // cols,),
        in_specs=[
            pl.BlockSpec((cols * n_ctx // width, chunk, LANES), lambda i: (i, 0, 0)),
            top,
            top,
            top,
            pl.BlockSpec((2 * HALO, cols), lambda i: (0, i)),
            pl.BlockSpec((1, cols), lambda i: (0, i)),
        ],
        out_specs=pl.BlockSpec((3, HALO, cols), lambda i: (0, 0, i)),
        out_shape=jax.ShapeDtypeStruct((3, HALO, width), bf16),
        compiler_params=pltpu.CompilerParams(vmem_limit_bytes=VMEM_LIMIT),
        name="heads",
    )(y, qc, kc, vc, *in_hbm(grad), skip)


def spread_kernel(
    y_ref, qc_ref, kc_ref, vc_ref, g_ref, skip_ref, taps_ref, out_ref, gq_ref, gk_ref, gv_ref, tail_ref, gf_ref, ext
):
    rows, cols = qc_ref.shape
    owners = y_ref.shape[0]
    half = cols // owners
    owned_groups = gf_ref.shape[0] // owners
    lines = [y_ref[o, 2 * half :, :].astype(f32)[:owned_groups] for o in range(owners)]
    gf_ref[...] = jnp.concatenate(lines, axis=0).astype(bf16)
    conv = tokens(y_ref, 0, half, rows)
    back = tokens(y_ref, half, half, rows)
    query_conv = qc_ref[...]
    mixed, gq, gk, gv = grads(
        conv, back, query_conv, kc_ref[...], vc_ref[...], g_ref[...].astype(f32), skip_ref[...]
    )
    out_ref[...] = (query_conv * mixed).astype(bf16)
    ext[rows:, :] = jnp.zeros((HALO, cols), f32)
    for which, (signal, target) in enumerate(((gq, gq_ref), (gk, gk_ref), (gv, gv_ref))):
        ext[:rows, :] = signal
        tail_ref[which] = signal[rows - TAIL :]
        target[...] = anti_sum(taps_ref, which, ext, rows).astype(bf16)


def spread(y, qc, kc, vc, grad, skip, taps_full):
    n_ctx, chunk, rows = y.shape
    width = qc.shape[1]
    cols = LANES
    tok = pl.BlockSpec((rows, cols), lambda i: (0, i))
    return pl.pallas_call(
        spread_kernel,
        grid=(width // cols,),
        in_specs=[
            pl.BlockSpec((cols * n_ctx // width, chunk, rows), lambda i: (i, 0, 0)),
            tok,
            tok,
            tok,
            tok,
            pl.BlockSpec((1, cols), lambda i: (0, i)),
            pl.BlockSpec((3, TAPS, cols), lambda i: (0, 0, i)),
        ],
        out_specs=[tok] * 4
        + [
            pl.BlockSpec((3, TAIL, cols), lambda i: (0, 0, i)),
            pl.BlockSpec((cols // GROUP, rows), lambda i: (i, 0)),
        ],
        out_shape=[jax.ShapeDtypeStruct((rows, width), bf16)] * 4
        + [jax.ShapeDtypeStruct((3, TAIL, width), f32), jax.ShapeDtypeStruct((width // GROUP, rows), bf16)],
        scratch_shapes=[pltpu.VMEM((rows + HALO, cols), f32)],
        compiler_params=pltpu.CompilerParams(vmem_limit_bytes=VMEM_LIMIT),
        cost_estimate=pl.CostEstimate(flops=12_000_000, bytes_accessed=8_000_000, transcendentals=0),
        name="spread",
    )(y, qc, kc, vc, *in_hbm(grad), skip, taps_full)


def tail_kernel(tail_ref, after_ref, taps_ref, gq_in, gk_in, gv_in, gq_ref, gk_ref, gv_ref, ext):
    for which, target in enumerate((gq_ref, gk_ref, gv_ref)):
        ext[:TAIL, :] = tail_ref[which]
        ext[TAIL:, :] = after_ref[which].astype(f32)
        target[...] = anti_sum(taps_ref, which, ext, TAIL).astype(bf16)


def tail(rims, after, taps_full, gq, gk, gv):
    rows, width = gq.shape
    last = rows // TAIL - 1
    strip = pl.BlockSpec((TAIL, width), lambda i: (last, 0))
    anywhere = pl.BlockSpec(memory_space=pl.ANY)
    return pl.pallas_call(
        tail_kernel,
        grid=(1,),
        in_specs=[
            pl.BlockSpec(rims.shape, lambda i: (0, 0, 0)),
            pl.BlockSpec(after.shape, lambda i: (0, 0, 0)),
            pl.BlockSpec(taps_full.shape, lambda i: (0, 0, 0)),
            anywhere,
            anywhere,
            anywhere,
        ],
        out_specs=[strip] * 3,
        out_shape=[jax.ShapeDtypeStruct(gq.shape, bf16)] * 3,
        scratch_shapes=[pltpu.VMEM((TAIL + HALO, width), f32)],
        input_output_aliases={3: 0, 4: 1, 5: 2},
        compiler_params=pltpu.CompilerParams(vmem_limit_bytes=VMEM_LIMIT),
        name="tail",
    )(rims, after, taps_full, gq, gk, gv)


def body(query_feats, key_feats, value_feats, short_taps, long_filter, skip_gain, out_grad):
    tok_rows, width = query_feats.shape
    n_ctx = lax.axis_size("ctx")
    length = tok_rows * n_ctx
    taps_full = jnp.repeat(short_taps, GROUP, axis=2)
    skip = skip_gain.reshape(1, width)
    rims = jnp.stack([a[tok_rows - HALO :] for a in (query_feats, key_feats, value_feats)])
    before = shifted(rims, "ctx", 1)
    x, qc, kc, vc = featurize(query_feats, key_feats, value_feats, out_grad, before, taps_full, long_filter.T, n_ctx)
    x = lax.all_to_all(x, "ctx", 0, 0, tiled=True)
    y = longconv(x, 1.0 / math.sqrt(length))
    y = lax.all_to_all(y, "ctx", 0, 0, tiled=True)
    after = shifted(heads(y, qc, kc, vc, out_grad, skip), "ctx", -1)
    mixed_out, gq, gk, gv, rims, gf = spread(y, qc, kc, vc, out_grad, skip, taps_full)
    gq, gk, gv = tail(rims, after, taps_full, gq, gk, gv)
    return (mixed_out, gq, gk, gv, gf.T)


def solution(mesh):
    in_specs = (
        P("ctx", "tp"),
        P("ctx", "tp"),
        P("ctx", "tp"),
        P(None, None, "tp"),
        P("ctx", "tp"),
        P("tp"),
        P("ctx", "tp"),
    )
    out_specs = (P("ctx", "tp"),) * 5
    return jax.shard_map(body, mesh=mesh, in_specs=in_specs, out_specs=out_specs, check_vma=False)
```

```python
import functools
import math

import jax
import jax.numpy as jnp
from jax import lax
from jax.experimental import pallas as pl
from jax.experimental.pallas import tpu as pltpu
from jax.sharding import PartitionSpec as P

D = 8192
SHORT_GROUPS = 512
GROUP = D // SHORT_GROUPS
TAPS = 7
HALO = 8
TAIL = 16
COLS = 256
CHUNK = 64
SPARE = 8
LANES = 128
VMEM_LIMIT = 26 * 1024 * 1024

f32 = jnp.float32
bf16 = jnp.bfloat16


def shifted(value, axis, steps):
    count = lax.axis_size(axis)
    initial, last = (max(0, -steps), min(count, count - steps))
    return lax.ppermute(value, axis, [(source, source + steps) for source in range(initial, last)])


def rims_kernel(q_ref, k_ref, v_ref, out_ref):
    for which, ref in enumerate((q_ref, k_ref, v_ref)):
        out_ref[which] = ref[...].astype(f32)[HALO:].astype(bf16)


def last_rows(query, key, value):
    rows, width = query.shape
    last = rows // TAIL - 1
    strip = pl.BlockSpec((TAIL, width), lambda i: (last, 0))
    return pl.pallas_call(
        rims_kernel,
        grid=(1,),
        in_specs=[strip] * 3,
        out_specs=pl.BlockSpec((3, HALO, width), lambda i: (0, 0, 0)),
        out_shape=jax.ShapeDtypeStruct((3, HALO, width), bf16),
        compiler_params=pltpu.CompilerParams(vmem_limit_bytes=VMEM_LIMIT),
        name="rims",
    )(*in_hbm(query, key, value))


def tap_rows(taps_ref, which, lanes):
    return [
        jnp.broadcast_to(taps_ref[HALO * which + j : HALO * which + j + 1, lanes], (8, LANES)) for j in range(TAPS)
    ]


def weighted(taps, pieces):
    total = None
    for tap, piece in zip(taps, pieces):
        term = piece.reshape(piece.shape[0] // 8, 8, LANES) * tap[None]
        total = term if total is None else total + term
    return total.reshape(-1, LANES)


def featurize_kernel(
    q_ref, k_ref, v_ref, g_ref, before_ref, taps_ref, f_ref, x_ref, qc_ref, kc_ref, vc_ref, wide_ref, wide, ext, gated, mix
):
    rows, cols = q_ref.shape
    owners = x_ref.shape[0]
    half = cols // owners
    owned_groups = f_ref.shape[0] // owners
    step = pl.program_id(0)

    @pl.when(step == 0)
    def _():
        groups = taps_ref.shape[2]
        shape = (groups, wide.shape[1])
        spot = lax.broadcasted_iota(jnp.int32, shape, 1) // GROUP == lax.broadcasted_iota(jnp.int32, shape, 0)
        for which in range(3):
            wide[HALO * which : HALO * which + TAPS, :] = jnp.dot(
                taps_ref[which], spot.astype(f32), precision=lax.Precision.HIGHEST, preferred_element_type=f32
            )
            wide[HALO * which + TAPS : HALO * (which + 1), :] = jnp.zeros((HALO - TAPS, wide.shape[1]), f32)

    wide_ref[...] = wide[:, pl.ds(pl.multiple_of(step * cols, cols), cols)]
    for which, ref in enumerate((q_ref, k_ref, v_ref)):
        ext[which, :HALO, :] = before_ref[which].astype(f32)
        ext[which, HALO:, :] = ref[...].astype(f32)
    for left in range(0, cols, LANES):
        lanes = slice(left, left + LANES)
        taps = [tap_rows(wide_ref, which, lanes) for which in range(3)]
        for lo in range(0, rows, CHUNK):
            part = slice(lo, lo + CHUNK)

            def conv(which):
                first = HALO + lo
                return weighted(taps[which], [ext[which, first - j : first - j + CHUNK, lanes] for j in range(TAPS)])

            key_conv = conv(1)
            kc_ref[part, lanes] = key_conv
            value_conv = conv(2)
            vc_ref[part, lanes] = value_conv
            gated[part, lanes] = (key_conv * value_conv).astype(bf16)
            query_conv = conv(0)
            qc_ref[part, lanes] = query_conv
            mix[part, lanes] = (g_ref[part, lanes].astype(f32) * query_conv).astype(bf16)
    x_ref[:, :half, :] = gated[...].T.reshape(owners, half, rows)
    x_ref[:, half : 2 * half, :] = mix[...].T.reshape(owners, half, rows)
    filt = f_ref[...].astype(f32)
    blank = jnp.zeros((SPARE - owned_groups, rows), f32)
    for owner in range(owners):
        lines = filt[owner * owned_groups : (owner + 1) * owned_groups]
        x_ref[owner, 2 * half :, :] = jnp.concatenate([lines, blank], axis=0).astype(bf16)


def in_hbm(*arrays):
    return [pltpu.with_memory_space_constraint(a, pltpu.HBM) for a in arrays]


def featurize(query, key, value, grad, before, short_taps, filt, n_ctx):
    rows, width = query.shape
    owned = width // n_ctx
    chunk = 2 * owned + SPARE
    cols = COLS
    tok = pl.BlockSpec((rows, cols), lambda i: (0, i))
    return pl.pallas_call(
        featurize_kernel,
        grid=(width // cols,),
        in_specs=[
            tok,
            tok,
            tok,
            tok,
            pl.BlockSpec((3, HALO, cols), lambda i: (0, 0, i)),
            pl.BlockSpec(short_taps.shape, lambda i: (0, 0, 0)),
            pl.BlockSpec((cols // GROUP, rows), lambda i: (i, 0)),
        ],
        out_specs=[
            pl.BlockSpec((cols // owned, chunk, rows), lambda i: (i, 0, 0)),
            tok,
            tok,
            tok,
            pl.BlockSpec((3 * HALO, cols), lambda i: (0, i)),
        ],
        out_shape=[
            pltpu.HBM((n_ctx, chunk, rows), bf16),
            jax.ShapeDtypeStruct((rows, width), f32),
            jax.ShapeDtypeStruct((rows, width), f32),
            jax.ShapeDtypeStruct((rows, width), f32),
            jax.ShapeDtypeStruct((3 * HALO, width), f32),
        ],
        scratch_shapes=[
            pltpu.VMEM((3 * HALO, width), f32),
            pltpu.VMEM((3, rows + HALO, cols), f32),
            pltpu.VMEM((rows, cols), bf16),
            pltpu.VMEM((rows, cols), bf16),
        ],
        compiler_params=pltpu.CompilerParams(vmem_limit_bytes=VMEM_LIMIT),
        name="featurize",
    )(*in_hbm(query, key, value, grad), before, short_taps, filt)


WIDE = 2048
BATCH = 4


def shift_right(value, steps):
    return value if steps == 0 else pltpu.roll(value, steps, axis=1)


def shift_left(value, steps):
    return value if steps == 0 else pltpu.roll(value, value.shape[1] - steps, axis=1)


def build_toeplitz(fpad, which, length, v8, toe):
    for lo in range(0, length, WIDE):
        wide = jnp.broadcast_to(fpad[pl.ds(which, 1), lo + LANES : lo + 2 * LANES + WIDE], (8, WIDE + LANES))
        row = lax.broadcasted_iota(jnp.int32, wide.shape, 0)
        for bit in (1, 2, 4):
            wide = jnp.where((row & bit) != 0, shift_right(wide, bit), wide)
        v8[:, lo + LANES : lo + LANES + WIDE] = wide[:, LANES:]
    v8[:, :LANES] = jnp.zeros((8, LANES), f32)
    toe[:, :LANES] = jnp.zeros((LANES, LANES), bf16)

    for lo in range(0, length, WIDE):
        wide = v8[:, lo : lo + LANES + WIDE]
        for p in range(0, LANES // 8, 2):
            pair = [shift_right(wide, 8 * (p + i))[:, LANES:] for i in range(2)]
            toe[8 * p : 8 * p + 16, lo + LANES : lo + LANES + WIDE] = jnp.concatenate(pair, axis=0).astype(bf16)


def fill_filter(x_ref, fpad):
    blocks, chunk, size = x_ref.shape
    fpad[:, : 2 * LANES] = jnp.zeros((SPARE, 2 * LANES), f32)
    for j in range(blocks):
        lo = 2 * LANES + size * j
        fpad[:, lo : lo + size] = x_ref[j, chunk - SPARE :, :].astype(f32)


def toeplitz_rows(toe, k, width):
    base = 2 * k * LANES
    return jnp.concatenate([toe[:, base + LANES : base + LANES + width], toe[:, base : base + width]], axis=0)


def forward_kernel(x_any, y_hbm, fpad, v8, toe, gpad, acc, y_ref, x_ref, sems, *, scale):
    g = pl.program_id(0)
    blocks, chunk, size = x_ref.shape
    rows = blocks * GROUP
    top = BATCH * GROUP

    @pl.when(g == 0)
    def _():
        half = (chunk - SPARE) // 2
        parts = (pl.ds(2 * half, SPARE), pl.ds(0, half))
        copies = [
            pltpu.make_async_copy(x_any.at[:, part, :], x_ref.at[:, part, :], sems.at[i])
            for i, part in enumerate(parts)
        ]
        for copy in copies:
            copy.start()
        copies[0].wait()
        fill_filter(x_ref, fpad)
        copies[1].wait()

    build_toeplitz(fpad, g, blocks * size, v8, toe)
    lines = pl.ds(pl.multiple_of(g * GROUP, GROUP), GROUP)
    gpad[:top, :] = jnp.zeros((top, size), bf16)
    gpad[top:, :] = x_ref[:, lines, :].reshape(rows, size)
    left = jnp.concatenate([gpad[top - GROUP * i : top - GROUP * i + rows, :] for i in range(BATCH)], axis=1)
    for kb in range(blocks // BATCH):
        first = top * kb
        right = jnp.concatenate([toeplitz_rows(toe, BATCH * kb + i, size) for i in range(BATCH)], axis=0)
        part = jnp.dot(left[: rows - first], right, preferred_element_type=f32)
        acc[first:, :] = part if kb == 0 else acc[first:, :] + part
    y_ref[:, lines, :] = (acc[...] * scale).astype(bf16).reshape(blocks, GROUP, size)
    out = pltpu.make_async_copy(y_ref.at[:, lines, :], y_hbm.at[:, lines, :], sems.at[2])
    out.start()
    out.wait()


def backward_kernel(x_any, y_hbm, fpad, v8, toe, gpad, zpad, acc, corr, fgrad, y_ref, x_ref, sems, *, scale):
    g = pl.program_id(0)
    blocks, chunk, size = x_ref.shape
    half = (chunk - SPARE) // 2
    length = blocks * size
    rows = blocks * GROUP
    near = rows // 2
    top = BATCH * GROUP

    @pl.when(g == 0)
    def _():
        x_in = pltpu.make_async_copy(x_any, x_ref, sems.at[2])
        x_in.start()
        x_in.wait()
        fill_filter(x_ref, fpad)
        fgrad[...] = jnp.zeros_like(fgrad)

    build_toeplitz(fpad, g, length, v8, toe)
    lines = pl.ds(pl.multiple_of(g * GROUP, GROUP), GROUP)
    back_lines = pl.ds(pl.multiple_of(half + g * GROUP, GROUP), GROUP)
    gpad[...] = x_ref[:, lines, :].reshape(rows, size)
    zpad[:rows, :] = x_ref[:, back_lines, :].reshape(rows, size)
    zpad[rows:, :] = jnp.zeros((zpad.shape[0] - rows, size), bf16)

    for kb in range(blocks // BATCH):
        first = top * kb
        count = rows - first
        right = toeplitz_rows(toe, BATCH * kb, BATCH * size)
        left = jnp.concatenate(
            [zpad[first + GROUP * i : first + GROUP * i + count, :] for i in range(BATCH)], axis=1
        )
        part = lax.dot_general(left, right, (((1,), (1,)), ((), ())), preferred_element_type=f32)
        acc[:count, :] = part if kb == 0 else acc[:count, :] + part
    y_ref[:, lines, :] = (acc[...] * scale).astype(bf16).reshape(blocks, GROUP, size)
    back_out = pltpu.make_async_copy(y_ref.at[:, lines, :], y_hbm.at[:, lines, :], sems.at[0])
    back_out.start()

    u_t = gpad[...].astype(f32).T.astype(bf16)
    for k in range(blocks):
        depth = rows if k < blocks // 2 else near
        corr[:, size * k : size * (k + 1)] = jnp.dot(
            u_t[:, :depth], zpad[GROUP * k : GROUP * k + depth, :], preferred_element_type=f32
        )
    corr[:, length:] = jnp.zeros((size, corr.shape[1] - length), f32)
    for lo in range(0, length, WIDE):
        total = None
        for p in reversed(range(LANES // 8)):
            part = (
                corr[8 * p : 8 * p + 8, lo : lo + WIDE + LANES]
                + corr[LANES + 8 * p : LANES + 8 * p + 8, lo + LANES : lo + WIDE + 2 * LANES]
            )
            total = part if total is None else shift_left(total, 8) + part
        row = lax.broadcasted_iota(jnp.int32, total.shape, 0)
        for bit in (4, 2, 1):
            total = jnp.where((row & bit) != 0, shift_left(total, bit), total)
        fgrad[pl.ds(g, 1), lo : lo + WIDE] = jnp.sum(total[:, :WIDE], axis=0, keepdims=True) * scale

    @pl.when(g == pl.num_programs(0) - 1)
    def _():
        for j in range(blocks):
            y_ref[j, half:, :] = fgrad[:, size * j : size * (j + 1)].astype(bf16)
        spare = pl.ds(half, SPARE)
        spare_out = pltpu.make_async_copy(y_ref.at[:, spare, :], y_hbm.at[:, spare, :], sems.at[1])
        spare_out.start()
        spare_out.wait()

    back_out.wait()


def longconv(kernel, x, out_rows, scratch, flops, scale, name):
    blocks, chunk, size = x.shape
    length = blocks * size
    shape = (blocks, out_rows, size)
    return pl.pallas_call(
        functools.partial(kernel, scale=scale),
        grid=((chunk - SPARE) // 2 // GROUP,),
        in_specs=[pl.BlockSpec(memory_space=pl.ANY)],
        out_specs=pl.BlockSpec(memory_space=pltpu.HBM),
        out_shape=pltpu.HBM(shape, bf16),
        scratch_shapes=[
            pltpu.VMEM((SPARE, length + 2 * LANES), f32),
            pltpu.VMEM((8, length + LANES), f32),
            pltpu.VMEM((LANES, length + LANES), bf16),
            *scratch,
        ],
        compiler_params=pltpu.CompilerParams(vmem_limit_bytes=VMEM_LIMIT),
        cost_estimate=pl.CostEstimate(flops=flops, bytes_accessed=2_000_000, transcendentals=0),
        name=name,
    )(*in_hbm(x))


def conv_forward(x, scale):
    blocks, chunk, size = x.shape
    half, rows = (chunk - SPARE) // 2, blocks * GROUP
    scratch = [
        pltpu.VMEM((rows + BATCH * GROUP, size), bf16),
        pltpu.VMEM((rows, size), f32),
        pltpu.VMEM((blocks, half, size), bf16),
        pltpu.VMEM(x.shape, bf16),
        pltpu.SemaphoreType.DMA((3,)),
    ]
    return longconv(forward_kernel, x, half, scratch, 2 * rows * rows * size * size // 64, scale, "conv_forward")


def conv_backward(x, scale):
    blocks, chunk, size = x.shape
    half, rows = (chunk - SPARE) // 2, blocks * GROUP
    length = blocks * size
    scratch = [
        pltpu.VMEM((rows, size), bf16),
        pltpu.VMEM((rows + rows // 2, size), bf16),
        pltpu.VMEM((rows, size), f32),
        pltpu.VMEM((size, length + 2 * LANES), f32),
        pltpu.VMEM((SPARE, length), f32),
        pltpu.VMEM((blocks, half + SPARE, size), bf16),
        pltpu.VMEM(x.shape, bf16),
        pltpu.SemaphoreType.DMA((3,)),
    ]
    flops = 4 * rows * rows * size * size // 32
    return longconv(backward_kernel, x, half + SPARE, scratch, flops, scale, "conv_backward")


def tokens(y_ref, count, lanes):
    owners = y_ref.shape[0]
    return y_ref[:, :count, :lanes].reshape(owners * count, lanes).T


def query_grads(conv, qc, kc, vc, grad, skip):
    mixed = conv + skip * (kc * vc).astype(bf16).astype(f32)
    return mixed, grad * mixed


def gate_grads(back, qc, kc, vc, grad, skip):
    grad_gate = back + skip * (grad * qc).astype(bf16).astype(f32)
    return grad_gate * vc, grad_gate * kc


def heads_kernel(y_ref, qc_ref, kc_ref, vc_ref, g_ref, skip_ref, out_ref, *, query):
    half = out_ref.shape[2] // y_ref.shape[0]
    y = tokens(y_ref, half, LANES).astype(f32)[:HALO]
    grad = g_ref[...].astype(f32)[:HALO]
    parts = (query_grads if query else gate_grads)(y, qc_ref[...], kc_ref[...], vc_ref[...], grad, skip_ref[...])
    for which in range(out_ref.shape[0]):
        out_ref[which] = parts[which + query].astype(bf16)


def heads(y, qc, kc, vc, grad, skip, query):
    n_ctx, chunk, rows = y.shape
    width = qc.shape[1]
    count = 1 if query else 2
    cols = 512
    top = pl.BlockSpec((HALO, cols), lambda i: (0, i))
    return pl.pallas_call(
        functools.partial(heads_kernel, query=query),
        grid=(width // cols,),
        in_specs=[
            pl.BlockSpec((cols * n_ctx // width, chunk, LANES), lambda i: (i, 0, 0)),
            top,
            top,
            top,
            pl.BlockSpec((2 * HALO, cols), lambda i: (0, i)),
            pl.BlockSpec((1, cols), lambda i: (0, i)),
        ],
        out_specs=pl.BlockSpec((count, HALO, cols), lambda i: (0, 0, i)),
        out_shape=jax.ShapeDtypeStruct((count, HALO, width), bf16),
        compiler_params=pltpu.CompilerParams(vmem_limit_bytes=VMEM_LIMIT),
        name="query_heads" if query else "gate_heads",
    )(y, qc, kc, vc, *in_hbm(grad), skip)


def spread_kernel(*refs, query):
    if query:
        y_ref, qc_ref, kc_ref, vc_ref, g_ref, skip_ref, taps_ref, after_ref, out_ref, gq_ref, ys, ext = refs
    else:
        y_ref, qc_ref, kc_ref, vc_ref, g_ref, skip_ref, taps_ref, gk_ref, gv_ref, tail_ref, gf_ref, ys, ext = refs
    rows, cols = qc_ref.shape
    owners = y_ref.shape[0]
    half = cols // owners
    count = ext.shape[0]
    ys[...] = tokens(y_ref, half, rows)
    for which in range(count):
        ext[which, rows:, :] = after_ref[0].astype(f32) if query else jnp.zeros((HALO, cols), f32)
    for left in range(0, cols, LANES):
        lanes = slice(left, left + LANES)
        taps = [tap_rows(taps_ref, which, lanes) for which in ((0,) if query else (1, 2))]
        skip = skip_ref[:, lanes]
        for lo in reversed(range(0, rows, CHUNK)):
            part = slice(lo, lo + CHUNK)
            qc = qc_ref[part, lanes]
            args = (ys[part, lanes].astype(f32), qc, kc_ref[part, lanes], vc_ref[part, lanes])
            grad = g_ref[part, lanes].astype(f32)
            if query:
                mixed, gq = query_grads(*args, grad, skip)
                out_ref[part, lanes] = (qc * mixed).astype(bf16)
                signals, targets = (gq,), (gq_ref,)
            else:
                signals, targets = gate_grads(*args, grad, skip), (gk_ref, gv_ref)
            for which in range(count):
                ext[which, part, lanes] = signals[which]
                pieces = [ext[which, lo + j : lo + j + CHUNK, lanes] for j in range(TAPS)]
                targets[which][part, lanes] = weighted(taps[which], pieces).astype(bf16)
    if not query:
        tail_ref[...] = ext[:, rows - TAIL : rows, :]
        owned_groups = gf_ref.shape[0] // owners
        lines = [y_ref[o, half:, :].astype(f32)[:owned_groups] for o in range(owners)]
        gf_ref[...] = jnp.concatenate(lines, axis=0).astype(bf16)


def spread(y, qc, kc, vc, grad, skip, taps_full, after=None):
    query = after is not None
    n_ctx, chunk, rows = y.shape
    width = qc.shape[1]
    cols = COLS
    count = 1 if query else 2
    tok = pl.BlockSpec((rows, cols), lambda i: (0, i))
    in_specs = [
        pl.BlockSpec((cols * n_ctx // width, chunk, rows), lambda i: (i, 0, 0)),
        tok,
        tok,
        tok,
        tok,
        pl.BlockSpec((1, cols), lambda i: (0, i)),
        pl.BlockSpec((3 * HALO, cols), lambda i: (0, i)),
    ]
    out_specs = [tok, tok]
    out_shape = [jax.ShapeDtypeStruct((rows, width), bf16)] * 2
    args = [y, qc, kc, vc, *in_hbm(grad), skip, taps_full]
    if query:
        in_specs.append(pl.BlockSpec((1, HALO, cols), lambda i: (0, 0, i)))
        args.append(after)
    else:
        out_specs += [
            pl.BlockSpec((2, TAIL, cols), lambda i: (0, 0, i)),
            pl.BlockSpec((cols // GROUP, rows), lambda i: (i, 0)),
        ]
        out_shape += [
            jax.ShapeDtypeStruct((2, TAIL, width), f32),
            jax.ShapeDtypeStruct((width // GROUP, rows), bf16),
        ]
    return pl.pallas_call(
        functools.partial(spread_kernel, query=query),
        grid=(width // cols,),
        in_specs=in_specs,
        out_specs=out_specs,
        out_shape=out_shape,
        scratch_shapes=[pltpu.VMEM((rows, cols), bf16), pltpu.VMEM((count, rows + HALO, cols), f32)],
        compiler_params=pltpu.CompilerParams(vmem_limit_bytes=VMEM_LIMIT),
        cost_estimate=pl.CostEstimate(flops=8_000_000, bytes_accessed=6_000_000, transcendentals=0),
        name="query_spread" if query else "gate_spread",
    )(*args)


def tail_kernel(tail_ref, after_ref, taps_ref, gk_in, gv_in, gk_ref, gv_ref, ext):
    ext[:, :TAIL, :] = tail_ref[...]
    ext[:, TAIL:, :] = after_ref[...].astype(f32)
    for which, target in enumerate((gk_ref, gv_ref)):
        for left in range(0, ext.shape[2], LANES):
            lanes = slice(left, left + LANES)
            pieces = [ext[which, j : j + TAIL, lanes] for j in range(TAPS)]
            target[:, lanes] = weighted(tap_rows(taps_ref, which + 1, lanes), pieces).astype(bf16)


def tail(rims, after, taps_full, gk, gv):
    rows, width = gk.shape
    last = rows // TAIL - 1
    strip = pl.BlockSpec((TAIL, width), lambda i: (last, 0))
    anywhere = pl.BlockSpec(memory_space=pl.ANY)
    return pl.pallas_call(
        tail_kernel,
        grid=(1,),
        in_specs=[
            pl.BlockSpec(rims.shape, lambda i: (0, 0, 0)),
            pl.BlockSpec(after.shape, lambda i: (0, 0, 0)),
            pl.BlockSpec(taps_full.shape, lambda i: (0, 0)),
            anywhere,
            anywhere,
        ],
        out_specs=[strip] * 2,
        out_shape=[jax.ShapeDtypeStruct(gk.shape, bf16)] * 2,
        scratch_shapes=[pltpu.VMEM((2, TAIL + HALO, width), f32)],
        input_output_aliases={3: 0, 4: 1},
        compiler_params=pltpu.CompilerParams(vmem_limit_bytes=VMEM_LIMIT),
        name="tail",
    )(rims, after, taps_full, gk, gv)


def body(query_feats, key_feats, value_feats, short_taps, long_filter, skip_gain, out_grad):
    tok_rows, width = query_feats.shape
    n_ctx = lax.axis_size("ctx")
    scale = 1.0 / math.sqrt(tok_rows * n_ctx)
    skip = skip_gain.reshape(1, width)
    before = shifted(last_rows(query_feats, key_feats, value_feats), "ctx", 1)
    x, qc, kc, vc, taps = featurize(
        query_feats, key_feats, value_feats, out_grad, before, short_taps, long_filter.T, n_ctx
    )
    x = lax.all_to_all(x, "ctx", 0, 0, tiled=True)
    conv = lax.all_to_all(conv_forward(x, scale), "ctx", 0, 0, tiled=True)
    back, conv = lax.optimization_barrier((conv_backward(x, scale), conv))
    back = lax.all_to_all(back, "ctx", 0, 0, tiled=True)
    after = shifted(heads(conv, qc, kc, vc, out_grad, skip, True), "ctx", -1)
    mixed_out, gq = spread(conv, qc, kc, vc, out_grad, skip, taps, after)
    back, mixed_out, gq = lax.optimization_barrier((back, mixed_out, gq))
    after = shifted(heads(back, qc, kc, vc, out_grad, skip, False), "ctx", -1)
    gk, gv, rims, gf = spread(back, qc, kc, vc, out_grad, skip, taps)
    gk, gv = tail(rims, after, taps, gk, gv)
    return (mixed_out, gq, gk, gv, gf.T)


def solution(mesh):
    in_specs = (
        P("ctx", "tp"),
        P("ctx", "tp"),
        P("ctx", "tp"),
        P(None, None, "tp"),
        P("ctx", "tp"),
        P("tp"),
        P("ctx", "tp"),
    )
    out_specs = (P("ctx", "tp"),) * 5
    return jax.shard_map(body, mesh=mesh, in_specs=in_specs, out_specs=out_specs, check_vma=False)
```

```python
import functools
import math

import jax
import jax.numpy as jnp
from jax import lax
from jax.experimental import pallas as pl
from jax.experimental.pallas import tpu as pltpu
from jax.sharding import PartitionSpec as P

D = 8192
SHORT_GROUPS = 512
GROUP = D // SHORT_GROUPS
TAPS = 7
HALO = 8
TAIL = 16
COLS = 256
CHUNK = 64
SPARE = 8
LANES = 128
VMEM_LIMIT = 30 * 1024 * 1024

f32 = jnp.float32
bf16 = jnp.bfloat16


def shifted(value, axis, steps):
    count = lax.axis_size(axis)
    initial, last = (max(0, -steps), min(count, count - steps))
    return lax.ppermute(value, axis, [(source, source + steps) for source in range(initial, last)])


def rims_kernel(q_ref, k_ref, v_ref, out_ref):
    for which, ref in enumerate((q_ref, k_ref, v_ref)):
        out_ref[which] = ref[...].astype(f32)[HALO:].astype(bf16)


def last_rows(query, key, value):
    rows, width = query.shape
    last = rows // TAIL - 1
    strip = pl.BlockSpec((TAIL, width), lambda i: (last, 0))
    return pl.pallas_call(
        rims_kernel,
        grid=(1,),
        in_specs=[strip] * 3,
        out_specs=pl.BlockSpec((3, HALO, width), lambda i: (0, 0, 0)),
        out_shape=jax.ShapeDtypeStruct((3, HALO, width), bf16),
        compiler_params=pltpu.CompilerParams(vmem_limit_bytes=VMEM_LIMIT),
        name="rims",
    )(*in_hbm(query, key, value))


def widen(short_taps):
    count, _, groups = short_taps.shape
    padded = jnp.pad(short_taps, ((0, 0), (0, HALO - TAPS), (0, 0)))
    return jnp.repeat(padded, GROUP, axis=2).reshape(count * HALO, groups * GROUP)


def tap_rows(taps_ref, which, lanes):
    return [
        jnp.broadcast_to(taps_ref[HALO * which + j : HALO * which + j + 1, lanes], (8, LANES)) for j in range(TAPS)
    ]


def weighted(taps, pieces):
    total = None
    for tap, piece in zip(taps, pieces):
        term = piece.reshape(piece.shape[0] // 8, 8, LANES) * tap[None]
        total = term if total is None else total + term
    return total.reshape(-1, LANES)


def featurize_kernel(
    q_ref, k_ref, v_ref, g_ref, before_ref, taps_ref, f_ref, x_ref, qc_ref, kc_ref, vc_ref, ext, gated, mix
):
    rows, cols = q_ref.shape
    owners = x_ref.shape[0]
    half = cols // owners
    owned_groups = half // GROUP
    start = pl.program_id(0) * cols
    here = pl.ds(pl.multiple_of(start, cols), cols)
    for which, ref in enumerate((q_ref, k_ref, v_ref)):
        ext[which, :HALO, :] = before_ref[which, :, here].astype(f32)
        ext[which, HALO:, :] = ref[...].astype(f32)
    for left in range(0, cols, LANES):
        lanes = slice(left, left + LANES)
        there = pl.ds(pl.multiple_of(start + left, LANES), LANES)
        taps = [tap_rows(taps_ref, which, there) for which in range(3)]
        for lo in range(0, rows, CHUNK):
            part = slice(lo, lo + CHUNK)

            def conv(which):
                first = HALO + lo
                return weighted(taps[which], [ext[which, first - j : first - j + CHUNK, lanes] for j in range(TAPS)])

            key_conv = conv(1)
            kc_ref[part, there] = key_conv
            value_conv = conv(2)
            vc_ref[part, there] = value_conv
            gated[part, lanes] = (key_conv * value_conv).astype(bf16)
            query_conv = conv(0)
            qc_ref[part, there] = query_conv
            mix[part, lanes] = (g_ref[part, lanes].astype(f32) * query_conv).astype(bf16)
    x_ref[:, :half, :] = gated[...].T.reshape(owners, half, rows)
    x_ref[:, half : 2 * half, :] = mix[...].T.reshape(owners, half, rows)
    lines = owners * owned_groups
    filt = f_ref[pl.ds(pl.multiple_of(pl.program_id(0) * lines, lines), lines), :].astype(f32)
    blank = jnp.zeros((SPARE - owned_groups, rows), f32)
    for owner in range(owners):
        mine = filt[owner * owned_groups : (owner + 1) * owned_groups]
        x_ref[owner, 2 * half :, :] = jnp.concatenate([mine, blank], axis=0).astype(bf16)


def in_hbm(*arrays):
    return [pltpu.with_memory_space_constraint(a, pltpu.HBM) for a in arrays]


def featurize(query, key, value, grad, before, taps_full, filt, n_ctx):
    rows, width = query.shape
    owned = width // n_ctx
    chunk = 2 * owned + SPARE
    cols = COLS
    tok = pl.BlockSpec((rows, cols), lambda i: (0, i))
    resident = pl.BlockSpec(memory_space=pltpu.VMEM)
    return pl.pallas_call(
        featurize_kernel,
        grid=(width // cols,),
        in_specs=[
            tok,
            tok,
            tok,
            tok,
            resident,
            resident,
            resident,
        ],
        out_specs=[
            pl.BlockSpec((cols // owned, chunk, rows), lambda i: (i, 0, 0)),
            resident,
            resident,
            resident,
        ],
        out_shape=[
            pltpu.HBM((n_ctx, chunk, rows), bf16),
            jax.ShapeDtypeStruct((rows, width), f32),
            jax.ShapeDtypeStruct((rows, width), f32),
            jax.ShapeDtypeStruct((rows, width), f32),
        ],
        scratch_shapes=[
            pltpu.VMEM((3, rows + HALO, cols), f32),
            pltpu.VMEM((rows, cols), bf16),
            pltpu.VMEM((rows, cols), bf16),
        ],
        compiler_params=pltpu.CompilerParams(vmem_limit_bytes=VMEM_LIMIT),
        name="featurize",
    )(*in_hbm(query, key, value, grad), before, taps_full, filt)


WIDE = 2048


def shift_left(value, steps):
    return value if steps == 0 else pltpu.roll(value, value.shape[1] - steps, axis=1)


def build_toeplitz(fpad, which, length, toe):
    toe[:, :LANES] = jnp.zeros((LANES, LANES), bf16)
    for lo in range(0, length, WIDE // 2):
        for p in range(0, LANES, 16):
            lanes = slice(lo + LANES, lo + 2 * LANES + WIDE // 2)
            wide = jnp.broadcast_to(fpad[pl.ds(which, 1), lanes], (16, WIDE // 2 + LANES))
            wide = pltpu.roll(wide, p, axis=1, stride=1, stride_axis=0)
            toe[p : p + 16, lo + LANES : lo + LANES + WIDE // 2] = wide[:, LANES:].astype(bf16)


def longconv_kernel(x_ref, y_hbm, fpad, toe, gpad, zpad, acc, corr, fgrad, y_ref, sems, *, scale):
    g = pl.program_id(0)
    blocks, chunk, size = x_ref.shape
    half = (chunk - SPARE) // 2
    length = blocks * size
    rows = blocks * GROUP
    group = GROUP
    groups = half // group
    batch = 2
    top = batch * group

    @pl.when(g == 0)
    def _():
        fpad[:, : 2 * LANES] = jnp.zeros((SPARE, 2 * LANES), f32)
        for j in range(blocks):
            lo = 2 * LANES + size * j
            fpad[:, lo : lo + size] = x_ref[j, 2 * half :, :].astype(f32)
        fgrad[...] = jnp.zeros_like(fgrad)

    build_toeplitz(fpad, g, length, toe)
    gpad[:top, :] = jnp.zeros((top, size), bf16)
    lines = pl.ds(pl.multiple_of(g * group, group), group)
    back_lines = pl.ds(pl.multiple_of(half + g * group, group), group)
    gpad[top:, :] = x_ref[:, lines, :].reshape(rows, size)
    zpad[:rows, :] = x_ref[:, back_lines, :].reshape(rows, size)
    zpad[rows:, :] = jnp.zeros((zpad.shape[0] - rows, size), bf16)

    u_t = gpad[top:, :].astype(f32).T.astype(bf16)
    near = rows // 2
    for k in range(blocks):
        depth = rows if k < blocks // 2 else near
        corr[:, size * k : size * (k + 1)] = jnp.dot(
            u_t[:, :depth], zpad[group * k : group * k + depth, :], preferred_element_type=f32
        )
    corr[:, length:] = jnp.zeros((size, corr.shape[1] - length), f32)
    for lo in range(0, length, WIDE):
        total = None
        for p in reversed(range(LANES // 8)):
            part = (
                corr[8 * p : 8 * p + 8, lo : lo + WIDE + LANES]
                + corr[LANES + 8 * p : LANES + 8 * p + 8, lo + LANES : lo + WIDE + 2 * LANES]
            )
            total = part if total is None else shift_left(total, 8) + part
        row = lax.broadcasted_iota(jnp.int32, total.shape, 0)
        for bit in (4, 2, 1):
            total = jnp.where((row & bit) != 0, shift_left(total, bit), total)
        fgrad[pl.ds(g, 1), lo : lo + WIDE] = jnp.sum(total[:, :WIDE], axis=0, keepdims=True) * scale

    def toeplitz_rows(k, width):
        base = 2 * k * LANES
        return jnp.concatenate(
            [toe[:, base + LANES : base + LANES + width], toe[:, base : base + width]], axis=0
        )

    left = jnp.concatenate([gpad[top - group * i : top - group * i + rows, :] for i in range(batch)], axis=1)
    for kb in range(blocks // batch):
        first = top * kb
        right = jnp.concatenate([toeplitz_rows(batch * kb + i, size) for i in range(batch)], axis=0)
        part = jnp.dot(left[: rows - first], right, preferred_element_type=f32)
        acc[first:, :] = part if kb == 0 else acc[first:, :] + part
    y_ref[:, lines, :] = (acc[...] * scale).astype(bf16).reshape(blocks, group, size)
    conv_out = pltpu.make_async_copy(y_ref.at[:, lines, :], y_hbm.at[:, lines, :], sems.at[g, 0])
    conv_out.start()

    for kb in range(blocks // batch):
        first = top * kb
        right = toeplitz_rows(batch * kb, batch * size)
        count = rows - first
        left = jnp.concatenate(
            [zpad[first + group * i : first + group * i + count, :] for i in range(batch)], axis=1
        )
        part = lax.dot_general(left, right, (((1,), (1,)), ((), ())), preferred_element_type=f32)
        acc[:count, :] = part if kb == 0 else acc[:count, :] + part
    y_ref[:, back_lines, :] = (acc[...] * scale).astype(bf16).reshape(blocks, group, size)
    back_out = pltpu.make_async_copy(y_ref.at[:, back_lines, :], y_hbm.at[:, back_lines, :], sems.at[g, 1])
    back_out.start()

    @pl.when(g == groups - 1)
    def _():
        for j in range(blocks):
            y_ref[j, 2 * half :, :] = fgrad[:, size * j : size * (j + 1)].astype(bf16)
        spare = pl.ds(2 * half, SPARE)
        spare_out = pltpu.make_async_copy(y_ref.at[:, spare, :], y_hbm.at[:, spare, :], sems.at[0, 2])
        spare_out.start()
        for i in range(groups):
            for k, first in enumerate((0, half)):
                part = pl.ds(first + i * group, group)
                pltpu.make_async_copy(y_ref.at[:, part, :], y_hbm.at[:, part, :], sems.at[i, k]).wait()
        spare_out.wait()


def longconv(x, scale):
    blocks, chunk, size = x.shape
    length = blocks * size
    rows = blocks * GROUP
    groups = (chunk - SPARE) // 2 // GROUP
    return pl.pallas_call(
        functools.partial(longconv_kernel, scale=scale),
        grid=(groups,),
        in_specs=[pl.BlockSpec(memory_space=pltpu.VMEM)],
        out_specs=pl.BlockSpec(memory_space=pltpu.HBM),
        out_shape=pltpu.HBM(x.shape, bf16),
        scratch_shapes=[
            pltpu.VMEM((SPARE, length + 2 * LANES), f32),
            pltpu.VMEM((LANES, length + LANES), bf16),
            pltpu.VMEM((rows + 2 * GROUP, size), bf16),
            pltpu.VMEM((rows + rows // 2, size), bf16),
            pltpu.VMEM((rows, size), f32),
            pltpu.VMEM((size, length + 2 * LANES), f32),
            pltpu.VMEM((SPARE, length), f32),
            pltpu.VMEM(x.shape, bf16),
            pltpu.SemaphoreType.DMA((groups, 3)),
        ],
        compiler_params=pltpu.CompilerParams(vmem_limit_bytes=VMEM_LIMIT),
        name="longconv",
    )(x)


def tokens(y_ref, lo, count, lanes):
    owners = y_ref.shape[0]
    return y_ref[:, lo : lo + count, :lanes].reshape(owners * count, lanes).T


def grads(conv, back, qc, kc, vc, grad, skip):
    gated = (kc * vc).astype(bf16).astype(f32)
    grad_mix = (grad * qc).astype(bf16).astype(f32)
    mixed = conv + skip * gated
    grad_gate = back + skip * grad_mix
    return mixed, grad * mixed, grad_gate * vc, grad_gate * kc


def heads_kernel(y_ref, qc_ref, kc_ref, vc_ref, g_ref, skip_ref, out_ref):
    half = (y_ref.shape[1] - SPARE) // 2
    conv = tokens(y_ref, 0, half, LANES).astype(f32)[:HALO]
    back = tokens(y_ref, half, half, LANES).astype(f32)[:HALO]
    grad = g_ref[...].astype(f32)[:HALO]
    _, gq, gk, gv = grads(conv, back, qc_ref[...], kc_ref[...], vc_ref[...], grad, skip_ref[...])
    out_ref[0] = gq.astype(bf16)
    out_ref[1] = gk.astype(bf16)
    out_ref[2] = gv.astype(bf16)


def heads(y, qc, kc, vc, grad, skip):
    n_ctx, chunk, rows = y.shape
    width = qc.shape[1]
    cols = 512
    top = pl.BlockSpec((HALO, cols), lambda i: (0, i))
    return pl.pallas_call(
        heads_kernel,
        grid=(width // cols,),
        in_specs=[
            pl.BlockSpec((cols * n_ctx // width, chunk, LANES), lambda i: (i, 0, 0)),
            top,
            top,
            top,
            pl.BlockSpec((2 * HALO, cols), lambda i: (0, i)),
            pl.BlockSpec((1, cols), lambda i: (0, i)),
        ],
        out_specs=pl.BlockSpec((3, HALO, cols), lambda i: (0, 0, i)),
        out_shape=jax.ShapeDtypeStruct((3, HALO, width), bf16),
        compiler_params=pltpu.CompilerParams(vmem_limit_bytes=VMEM_LIMIT),
        name="heads",
    )(y, qc, kc, vc, *in_hbm(grad), skip)


def spread_kernel(
    y_ref, qc_ref, kc_ref, vc_ref, g_ref, skip_ref, taps_ref, out_ref, gq_ref, gk_ref, gv_ref, tail_ref, gf_ref, conv, back, ext
):
    rows, cols = g_ref.shape
    half = (y_ref.shape[1] - SPARE) // 2
    owners = cols // half
    owned_groups = gf_ref.shape[0] // owners
    step = pl.program_id(0)
    y_ref = y_ref.at[pl.ds(step * owners, owners)]
    lines = [y_ref[o, 2 * half :, :].astype(f32)[:owned_groups] for o in range(owners)]
    gf_ref[...] = jnp.concatenate(lines, axis=0).astype(bf16)
    conv[...] = tokens(y_ref, 0, half, rows)
    back[...] = tokens(y_ref, half, half, rows)
    for which in range(3):
        ext[which, rows:, :] = jnp.zeros((HALO, cols), f32)
    for left in range(0, cols, LANES):
        lanes = slice(left, left + LANES)
        there = pl.ds(pl.multiple_of(step * cols + left, LANES), LANES)
        taps = [tap_rows(taps_ref, which, there) for which in range(3)]
        for lo in reversed(range(0, rows, CHUNK)):
            part = slice(lo, lo + CHUNK)
            qc = qc_ref[part, there]
            mixed, *signals = grads(
                conv[part, lanes].astype(f32),
                back[part, lanes].astype(f32),
                qc,
                kc_ref[part, there],
                vc_ref[part, there],
                g_ref[part, lanes].astype(f32),
                skip_ref[:, there],
            )
            out_ref[part, lanes] = (qc * mixed).astype(bf16)
            for which, target in enumerate((gq_ref, gk_ref, gv_ref)):
                ext[which, part, lanes] = signals[which]
                pieces = [ext[which, lo + j : lo + j + CHUNK, lanes] for j in range(TAPS)]
                target[part, lanes] = weighted(taps[which], pieces).astype(bf16)
    tail_ref[...] = ext[:, rows - TAIL : rows, :]


def spread(y, qc, kc, vc, grad, skip, taps_full):
    n_ctx, chunk, rows = y.shape
    width = qc.shape[1]
    cols = COLS
    tok = pl.BlockSpec((rows, cols), lambda i: (0, i))
    resident = pl.BlockSpec(memory_space=pltpu.VMEM)
    return pl.pallas_call(
        spread_kernel,
        grid=(width // cols,),
        in_specs=[resident] * 4 + [tok] + [resident] * 2,
        out_specs=[tok] * 4
        + [
            pl.BlockSpec((3, TAIL, cols), lambda i: (0, 0, i)),
            pl.BlockSpec((cols // GROUP, rows), lambda i: (i, 0)),
        ],
        out_shape=[jax.ShapeDtypeStruct((rows, width), bf16)] * 4
        + [jax.ShapeDtypeStruct((3, TAIL, width), f32), jax.ShapeDtypeStruct((width // GROUP, rows), bf16)],
        scratch_shapes=[
            pltpu.VMEM((rows, cols), bf16),
            pltpu.VMEM((rows, cols), bf16),
            pltpu.VMEM((3, rows + HALO, cols), f32),
        ],
        compiler_params=pltpu.CompilerParams(vmem_limit_bytes=VMEM_LIMIT),
        cost_estimate=pl.CostEstimate(flops=12_000_000, bytes_accessed=8_000_000, transcendentals=0),
        name="spread",
    )(y, qc, kc, vc, *in_hbm(grad), skip, taps_full)


def tail_kernel(tail_ref, after_ref, taps_ref, gq_in, gk_in, gv_in, gq_ref, gk_ref, gv_ref, ext):
    ext[:, :TAIL, :] = tail_ref[...]
    ext[:, TAIL:, :] = after_ref[...].astype(f32)
    for which, target in enumerate((gq_ref, gk_ref, gv_ref)):
        for left in range(0, ext.shape[2], LANES):
            lanes = slice(left, left + LANES)
            pieces = [ext[which, j : j + TAIL, lanes] for j in range(TAPS)]
            target[:, lanes] = weighted(tap_rows(taps_ref, which, lanes), pieces).astype(bf16)


def tail(rims, after, taps_full, gq, gk, gv):
    rows, width = gq.shape
    last = rows // TAIL - 1
    strip = pl.BlockSpec((TAIL, width), lambda i: (last, 0))
    anywhere = pl.BlockSpec(memory_space=pl.ANY)
    return pl.pallas_call(
        tail_kernel,
        grid=(1,),
        in_specs=[
            pl.BlockSpec(rims.shape, lambda i: (0, 0, 0)),
            pl.BlockSpec(after.shape, lambda i: (0, 0, 0)),
            pl.BlockSpec(taps_full.shape, lambda i: (0, 0)),
            anywhere,
            anywhere,
            anywhere,
        ],
        out_specs=[strip] * 3,
        out_shape=[jax.ShapeDtypeStruct(gq.shape, bf16)] * 3,
        scratch_shapes=[pltpu.VMEM((3, TAIL + HALO, width), f32)],
        input_output_aliases={3: 0, 4: 1, 5: 2},
        compiler_params=pltpu.CompilerParams(vmem_limit_bytes=VMEM_LIMIT),
        name="tail",
    )(rims, after, taps_full, gq, gk, gv)


def body(query_feats, key_feats, value_feats, short_taps, long_filter, skip_gain, out_grad):
    tok_rows, width = query_feats.shape
    n_ctx = lax.axis_size("ctx")
    length = tok_rows * n_ctx
    taps_full = widen(short_taps)
    skip = skip_gain.reshape(1, width)
    before = shifted(last_rows(query_feats, key_feats, value_feats), "ctx", 1)
    x, qc, kc, vc = featurize(query_feats, key_feats, value_feats, out_grad, before, taps_full, long_filter.T, n_ctx)
    x = lax.all_to_all(x, "ctx", 0, 0, tiled=True)
    y = longconv(x, 1.0 / math.sqrt(length))
    y = lax.all_to_all(y, "ctx", 0, 0, tiled=True)
    after = shifted(heads(y, qc, kc, vc, out_grad, skip), "ctx", -1)
    mixed_out, gq, gk, gv, rims, gf = spread(y, qc, kc, vc, out_grad, skip, taps_full)
    gq, gk, gv = tail(rims, after, taps_full, gq, gk, gv)
    return (mixed_out, gq, gk, gv, gf.T)


def solution(mesh):
    in_specs = (
        P("ctx", "tp"),
        P("ctx", "tp"),
        P("ctx", "tp"),
        P(None, None, "tp"),
        P("ctx", "tp"),
        P("tp"),
        P("ctx", "tp"),
    )
    out_specs = (P("ctx", "tp"),) * 5
    return jax.shard_map(body, mesh=mesh, in_specs=in_specs, out_specs=out_specs, check_vma=False)
```

```python
import functools
import math

import jax
import jax.numpy as jnp
from jax import lax
from jax.experimental import pallas as pl
from jax.experimental.pallas import tpu as pltpu
from jax.sharding import PartitionSpec as P

D = 8192
SHORT_GROUPS = 512
GROUP = D // SHORT_GROUPS
TAPS = 7
HALO = 8
TAIL = 16
COLS = 256
CHUNK = 64
SPARE = 8
HALVES = 2
LANES = 128
VMEM_LIMIT = 30 * 1024 * 1024

f32 = jnp.float32
bf16 = jnp.bfloat16


def shifted(value, axis, steps):
    count = lax.axis_size(axis)
    initial, last = (max(0, -steps), min(count, count - steps))
    return lax.ppermute(value, axis, [(source, source + steps) for source in range(initial, last)])


def rims_kernel(q_ref, k_ref, v_ref, out_ref):
    for which, ref in enumerate((q_ref, k_ref, v_ref)):
        out_ref[which] = ref[...].astype(f32)[HALO:].astype(bf16)


def last_rows(query, key, value):
    rows, width = query.shape
    last = rows // TAIL - 1
    strip = pl.BlockSpec((TAIL, width), lambda i: (last, 0))
    return pl.pallas_call(
        rims_kernel,
        grid=(1,),
        in_specs=[strip] * 3,
        out_specs=pl.BlockSpec((3, HALO, width), lambda i: (0, 0, 0)),
        out_shape=jax.ShapeDtypeStruct((3, HALO, width), bf16),
        compiler_params=pltpu.CompilerParams(vmem_limit_bytes=VMEM_LIMIT),
        name="rims",
    )(*in_hbm(query, key, value))


def widen(short_taps):
    count, _, groups = short_taps.shape
    padded = jnp.pad(short_taps, ((0, 0), (0, HALO - TAPS), (0, 0)))
    return jnp.repeat(padded, GROUP, axis=2).reshape(count * HALO, groups * GROUP)


def tap_rows(taps_ref, which, lanes):
    return [
        jnp.broadcast_to(taps_ref[HALO * which + j : HALO * which + j + 1, lanes], (8, LANES)) for j in range(TAPS)
    ]


def weighted(taps, pieces):
    total = None
    for tap, piece in zip(taps, pieces):
        term = piece.reshape(piece.shape[0] // 8, 8, LANES) * tap[None]
        total = term if total is None else total + term
    return total.reshape(-1, LANES)


def featurize_kernel(
    q_ref, k_ref, v_ref, g_ref, before_ref, taps_ref, f_ref, x_ref, qc_ref, kc_ref, vc_ref, ext, gated, mix
):
    rows, cols = q_ref.shape
    owners = x_ref.shape[0]
    half = cols // owners
    owned_groups = half // GROUP
    start = pl.program_id(0) * cols
    here = pl.ds(pl.multiple_of(start, cols), cols)
    for which, ref in enumerate((q_ref, k_ref, v_ref)):
        ext[which, :HALO, :] = before_ref[which, :, here].astype(f32)
        ext[which, HALO:, :] = ref[...].astype(f32)
    for left in range(0, cols, LANES):
        lanes = slice(left, left + LANES)
        there = pl.ds(pl.multiple_of(start + left, LANES), LANES)
        taps = [tap_rows(taps_ref, which, there) for which in range(3)]
        for lo in range(0, rows, CHUNK):
            part = slice(lo, lo + CHUNK)

            def conv(which):
                first = HALO + lo
                return weighted(taps[which], [ext[which, first - j : first - j + CHUNK, lanes] for j in range(TAPS)])

            key_conv = conv(1)
            kc_ref[part, there] = key_conv
            value_conv = conv(2)
            vc_ref[part, there] = value_conv
            gated[part, lanes] = (key_conv * value_conv).astype(bf16)
            query_conv = conv(0)
            qc_ref[part, there] = query_conv
            mix[part, lanes] = (g_ref[part, lanes].astype(f32) * query_conv).astype(bf16)
    for which, signal in enumerate((gated, mix)):
        for part in range(HALVES):
            first = (HALVES * which + part) * half
            piece = signal[LANES * part : LANES * (part + 1), :].T
            x_ref[:, first : first + half, :] = piece.reshape(owners, half, LANES)
    lines = owners * owned_groups
    filt = f_ref[pl.ds(pl.multiple_of(pl.program_id(0) * lines, lines), lines), :].astype(f32)
    blank = jnp.zeros((SPARE - HALVES * owned_groups, LANES), f32)
    for owner in range(owners):
        mine = filt[owner * owned_groups : (owner + 1) * owned_groups]
        pieces = [mine[:, LANES * part : LANES * (part + 1)] for part in range(HALVES)]
        x_ref[owner, 2 * HALVES * half :, :] = jnp.concatenate([*pieces, blank], axis=0).astype(bf16)


def in_hbm(*arrays):
    return [pltpu.with_memory_space_constraint(a, pltpu.HBM) for a in arrays]


def featurize(query, key, value, grad, before, taps_full, filt, n_ctx):
    rows, width = query.shape
    owned = width // n_ctx
    chunk = 2 * HALVES * owned + SPARE
    cols = COLS
    tok = pl.BlockSpec((rows, cols), lambda i: (0, i))
    resident = pl.BlockSpec(memory_space=pltpu.VMEM)
    return pl.pallas_call(
        featurize_kernel,
        grid=(width // cols,),
        in_specs=[
            tok,
            tok,
            tok,
            tok,
            resident,
            resident,
            resident,
        ],
        out_specs=[
            pl.BlockSpec((cols // owned, chunk, LANES), lambda i: (i, 0, 0)),
            resident,
            resident,
            resident,
        ],
        out_shape=[
            pltpu.HBM((n_ctx, chunk, LANES), bf16),
            jax.ShapeDtypeStruct((rows, width), f32),
            jax.ShapeDtypeStruct((rows, width), f32),
            jax.ShapeDtypeStruct((rows, width), f32),
        ],
        scratch_shapes=[
            pltpu.VMEM((3, rows + HALO, cols), f32),
            pltpu.VMEM((rows, cols), bf16),
            pltpu.VMEM((rows, cols), bf16),
        ],
        compiler_params=pltpu.CompilerParams(vmem_limit_bytes=VMEM_LIMIT),
        name="featurize",
    )(*in_hbm(query, key, value, grad), before, taps_full, filt)


WIDE = 2048


def shift_left(value, steps):
    return value if steps == 0 else pltpu.roll(value, value.shape[1] - steps, axis=1)


def build_toeplitz(fpad, which, length, toe):
    toe[:, :LANES] = jnp.zeros((LANES, LANES), bf16)
    for lo in range(0, length, WIDE // 2):
        for p in range(0, LANES, 16):
            lanes = slice(lo + LANES, lo + 2 * LANES + WIDE // 2)
            wide = jnp.broadcast_to(fpad[pl.ds(which, 1), lanes], (16, WIDE // 2 + LANES))
            wide = pltpu.roll(wide, p, axis=1, stride=1, stride_axis=0)
            toe[p : p + 16, lo + LANES : lo + LANES + WIDE // 2] = wide[:, LANES:].astype(bf16)


def longconv_kernel(x_ref, y_hbm, fpad, toe, gpad, zpad, acc, corr, fgrad, y_ref, sems, *, scale):
    g = pl.program_id(0)
    blocks, chunk, _ = x_ref.shape
    size = HALVES * LANES
    half = (chunk - SPARE) // (2 * HALVES)
    length = blocks * size
    rows = blocks * GROUP
    group = GROUP
    groups = half // group
    batch = 2
    top = batch * group

    @pl.when(g == 0)
    def _():
        fpad[:, : 2 * LANES] = jnp.zeros((SPARE, 2 * LANES), f32)
        for j in range(blocks):
            spare = x_ref[j, 2 * HALVES * half :, :].astype(f32)
            for part in range(HALVES):
                lo = 2 * LANES + size * j + LANES * part
                fpad[:groups, lo : lo + LANES] = spare[groups * part : groups * (part + 1)]
        fgrad[...] = jnp.zeros_like(fgrad)

    build_toeplitz(fpad, g, length, toe)
    gpad[:top, :] = jnp.zeros((top, size), bf16)

    def lines(which, part):
        return pl.ds(pl.multiple_of((HALVES * which + part) * half + g * group, group), group)

    def put(which):
        for part in range(HALVES):
            piece = (acc[:, LANES * part : LANES * (part + 1)] * scale).astype(bf16)
            place = lines(which, part)
            y_ref[:, place, :] = piece.reshape(blocks, group, LANES)
            copy(g, which, part).start()

    def copy(i, which, part):
        place = pl.ds(pl.multiple_of((HALVES * which + part) * half + i * group, group), group)
        return pltpu.make_async_copy(
            y_ref.at[:, place, :], y_hbm.at[:, place, :], sems.at[i, HALVES * which + part]
        )

    for part in range(HALVES):
        lanes = slice(LANES * part, LANES * (part + 1))
        gpad[top:, lanes] = x_ref[:, lines(0, part), :].reshape(rows, LANES)
        zpad[:rows, lanes] = x_ref[:, lines(1, part), :].reshape(rows, LANES)
    zpad[rows:, :] = jnp.zeros((zpad.shape[0] - rows, size), bf16)

    u_t = gpad[top:, :].astype(f32).T.astype(bf16)
    near = rows // 2
    for k in range(blocks):
        depth = rows if k < blocks // 2 else near
        corr[:, size * k : size * (k + 1)] = jnp.dot(
            u_t[:, :depth], zpad[group * k : group * k + depth, :], preferred_element_type=f32
        )
    corr[:, length:] = jnp.zeros((size, corr.shape[1] - length), f32)
    for lo in range(0, length, WIDE):
        total = None
        for p in reversed(range(LANES // 8)):
            part = (
                corr[8 * p : 8 * p + 8, lo : lo + WIDE + LANES]
                + corr[LANES + 8 * p : LANES + 8 * p + 8, lo + LANES : lo + WIDE + 2 * LANES]
            )
            total = part if total is None else shift_left(total, 8) + part
        row = lax.broadcasted_iota(jnp.int32, total.shape, 0)
        for bit in (4, 2, 1):
            total = jnp.where((row & bit) != 0, shift_left(total, bit), total)
        fgrad[pl.ds(g, 1), lo : lo + WIDE] = jnp.sum(total[:, :WIDE], axis=0, keepdims=True) * scale

    def toeplitz_rows(k, width):
        base = 2 * k * LANES
        return jnp.concatenate(
            [toe[:, base + LANES : base + LANES + width], toe[:, base : base + width]], axis=0
        )

    left = jnp.concatenate([gpad[top - group * i : top - group * i + rows, :] for i in range(batch)], axis=1)
    for kb in range(blocks // batch):
        first = top * kb
        right = jnp.concatenate([toeplitz_rows(batch * kb + i, size) for i in range(batch)], axis=0)
        part = jnp.dot(left[: rows - first], right, preferred_element_type=f32)
        acc[first:, :] = part if kb == 0 else acc[first:, :] + part
    put(0)

    for kb in range(blocks // batch):
        first = top * kb
        right = toeplitz_rows(batch * kb, batch * size)
        count = rows - first
        left = jnp.concatenate(
            [zpad[first + group * i : first + group * i + count, :] for i in range(batch)], axis=1
        )
        part = lax.dot_general(left, right, (((1,), (1,)), ((), ())), preferred_element_type=f32)
        acc[:count, :] = part if kb == 0 else acc[:count, :] + part
    put(1)

    @pl.when(g == groups - 1)
    def _():
        blank = jnp.zeros((SPARE - HALVES * groups, LANES), f32)
        for j in range(blocks):
            starts = [size * j + LANES * part for part in range(HALVES)]
            pieces = [fgrad[:groups, lo : lo + LANES] for lo in starts]
            y_ref[j, 2 * HALVES * half :, :] = jnp.concatenate([*pieces, blank], axis=0).astype(bf16)
        spare = pl.ds(2 * HALVES * half, SPARE)
        spare_out = pltpu.make_async_copy(
            y_ref.at[:, spare, :], y_hbm.at[:, spare, :], sems.at[0, 2 * HALVES]
        )
        spare_out.start()
        for i in range(groups):
            for which in range(2):
                for part in range(HALVES):
                    copy(i, which, part).wait()
        spare_out.wait()


def longconv(x, scale):
    blocks, chunk, _ = x.shape
    size = HALVES * LANES
    length = blocks * size
    rows = blocks * GROUP
    groups = (chunk - SPARE) // (2 * HALVES) // GROUP
    return pl.pallas_call(
        functools.partial(longconv_kernel, scale=scale),
        grid=(groups,),
        in_specs=[pl.BlockSpec(memory_space=pltpu.VMEM)],
        out_specs=pl.BlockSpec(memory_space=pltpu.HBM),
        out_shape=pltpu.HBM(x.shape, bf16),
        scratch_shapes=[
            pltpu.VMEM((SPARE, length + 2 * LANES), f32),
            pltpu.VMEM((LANES, length + LANES), bf16),
            pltpu.VMEM((rows + 2 * GROUP, size), bf16),
            pltpu.VMEM((rows + rows // 2, size), bf16),
            pltpu.VMEM((rows, size), f32),
            pltpu.VMEM((size, length + 2 * LANES), f32),
            pltpu.VMEM((SPARE, length), f32),
            pltpu.VMEM(x.shape, bf16),
            pltpu.SemaphoreType.DMA((groups, 2 * HALVES + 1)),
        ],
        compiler_params=pltpu.CompilerParams(vmem_limit_bytes=VMEM_LIMIT),
        name="longconv",
    )(x)


def tokens(y_ref, block, count):
    owners = y_ref.shape[0]
    return y_ref[:, block * count : (block + 1) * count, :].reshape(owners * count, LANES).T


def grads(conv, back, qc, kc, vc, grad, skip):
    gated = (kc * vc).astype(bf16).astype(f32)
    grad_mix = (grad * qc).astype(bf16).astype(f32)
    mixed = conv + skip * gated
    grad_gate = back + skip * grad_mix
    return mixed, grad * mixed, grad_gate * vc, grad_gate * kc


def heads_kernel(y_ref, qc_ref, kc_ref, vc_ref, g_ref, skip_ref, out_ref):
    half = (y_ref.shape[1] - SPARE) // (2 * HALVES)
    conv = tokens(y_ref, 0, half).astype(f32)[:HALO]
    back = tokens(y_ref, HALVES, half).astype(f32)[:HALO]
    grad = g_ref[...].astype(f32)[:HALO]
    _, gq, gk, gv = grads(conv, back, qc_ref[...], kc_ref[...], vc_ref[...], grad, skip_ref[...])
    out_ref[0] = gq.astype(bf16)
    out_ref[1] = gk.astype(bf16)
    out_ref[2] = gv.astype(bf16)


def heads(y, qc, kc, vc, grad, skip):
    n_ctx, chunk, _ = y.shape
    width = qc.shape[1]
    cols = 512
    top = pl.BlockSpec((HALO, cols), lambda i: (0, i))
    return pl.pallas_call(
        heads_kernel,
        grid=(width // cols,),
        in_specs=[
            pl.BlockSpec((cols * n_ctx // width, chunk, LANES), lambda i: (i, 0, 0)),
            top,
            top,
            top,
            pl.BlockSpec((2 * HALO, cols), lambda i: (0, i)),
            pl.BlockSpec((1, cols), lambda i: (0, i)),
        ],
        out_specs=pl.BlockSpec((3, HALO, cols), lambda i: (0, 0, i)),
        out_shape=jax.ShapeDtypeStruct((3, HALO, width), bf16),
        compiler_params=pltpu.CompilerParams(vmem_limit_bytes=VMEM_LIMIT),
        name="heads",
    )(y, qc, kc, vc, *in_hbm(grad), skip)


def spread_kernel(
    y_ref, qc_ref, kc_ref, vc_ref, g_ref, skip_ref, taps_ref, out_ref, gq_ref, gk_ref, gv_ref, tail_ref, gf_ref, conv, back, ext
):
    rows, cols = g_ref.shape
    half = (y_ref.shape[1] - SPARE) // (2 * HALVES)
    owners = cols // half
    owned_groups = gf_ref.shape[0] // owners
    step = pl.program_id(0)
    y_ref = y_ref.at[pl.ds(step * owners, owners)]
    lines = []
    for owner in range(owners):
        spare = y_ref[owner, 2 * HALVES * half :, :].astype(f32)
        pieces = [spare[owned_groups * part : owned_groups * (part + 1)] for part in range(HALVES)]
        lines.append(jnp.concatenate(pieces, axis=1))
    gf_ref[...] = jnp.concatenate(lines, axis=0).astype(bf16)
    for part in range(HALVES):
        conv[LANES * part : LANES * (part + 1), :] = tokens(y_ref, part, half)
        back[LANES * part : LANES * (part + 1), :] = tokens(y_ref, HALVES + part, half)
    for which in range(3):
        ext[which, rows:, :] = jnp.zeros((HALO, cols), f32)
    for left in range(0, cols, LANES):
        lanes = slice(left, left + LANES)
        there = pl.ds(pl.multiple_of(step * cols + left, LANES), LANES)
        taps = [tap_rows(taps_ref, which, there) for which in range(3)]
        for lo in reversed(range(0, rows, CHUNK)):
            part = slice(lo, lo + CHUNK)
            qc = qc_ref[part, there]
            mixed, *signals = grads(
                conv[part, lanes].astype(f32),
                back[part, lanes].astype(f32),
                qc,
                kc_ref[part, there],
                vc_ref[part, there],
                g_ref[part, lanes].astype(f32),
                skip_ref[:, there],
            )
            out_ref[part, lanes] = (qc * mixed).astype(bf16)
            for which, target in enumerate((gq_ref, gk_ref, gv_ref)):
                ext[which, part, lanes] = signals[which]
                pieces = [ext[which, lo + j : lo + j + CHUNK, lanes] for j in range(TAPS)]
                target[part, lanes] = weighted(taps[which], pieces).astype(bf16)
    tail_ref[...] = ext[:, rows - TAIL : rows, :]


def spread(y, qc, kc, vc, grad, skip, taps_full):
    rows, width = qc.shape
    cols = COLS
    tok = pl.BlockSpec((rows, cols), lambda i: (0, i))
    resident = pl.BlockSpec(memory_space=pltpu.VMEM)
    return pl.pallas_call(
        spread_kernel,
        grid=(width // cols,),
        in_specs=[resident] * 4 + [tok] + [resident] * 2,
        out_specs=[tok] * 4
        + [
            pl.BlockSpec((3, TAIL, cols), lambda i: (0, 0, i)),
            pl.BlockSpec((cols // GROUP, rows), lambda i: (i, 0)),
        ],
        out_shape=[jax.ShapeDtypeStruct((rows, width), bf16)] * 4
        + [jax.ShapeDtypeStruct((3, TAIL, width), f32), jax.ShapeDtypeStruct((width // GROUP, rows), bf16)],
        scratch_shapes=[
            pltpu.VMEM((rows, cols), bf16),
            pltpu.VMEM((rows, cols), bf16),
            pltpu.VMEM((3, rows + HALO, cols), f32),
        ],
        compiler_params=pltpu.CompilerParams(vmem_limit_bytes=VMEM_LIMIT),
        cost_estimate=pl.CostEstimate(flops=12_000_000, bytes_accessed=8_000_000, transcendentals=0),
        name="spread",
    )(y, qc, kc, vc, *in_hbm(grad), skip, taps_full)


def tail_kernel(tail_ref, after_ref, taps_ref, gq_in, gk_in, gv_in, gq_ref, gk_ref, gv_ref, ext):
    ext[:, :TAIL, :] = tail_ref[...]
    ext[:, TAIL:, :] = after_ref[...].astype(f32)
    for which, target in enumerate((gq_ref, gk_ref, gv_ref)):
        for left in range(0, ext.shape[2], LANES):
            lanes = slice(left, left + LANES)
            pieces = [ext[which, j : j + TAIL, lanes] for j in range(TAPS)]
            target[:, lanes] = weighted(tap_rows(taps_ref, which, lanes), pieces).astype(bf16)


def tail(rims, after, taps_full, gq, gk, gv):
    rows, width = gq.shape
    last = rows // TAIL - 1
    strip = pl.BlockSpec((TAIL, width), lambda i: (last, 0))
    anywhere = pl.BlockSpec(memory_space=pl.ANY)
    return pl.pallas_call(
        tail_kernel,
        grid=(1,),
        in_specs=[
            pl.BlockSpec(rims.shape, lambda i: (0, 0, 0)),
            pl.BlockSpec(after.shape, lambda i: (0, 0, 0)),
            pl.BlockSpec(taps_full.shape, lambda i: (0, 0)),
            anywhere,
            anywhere,
            anywhere,
        ],
        out_specs=[strip] * 3,
        out_shape=[jax.ShapeDtypeStruct(gq.shape, bf16)] * 3,
        scratch_shapes=[pltpu.VMEM((3, TAIL + HALO, width), f32)],
        input_output_aliases={3: 0, 4: 1, 5: 2},
        compiler_params=pltpu.CompilerParams(vmem_limit_bytes=VMEM_LIMIT),
        name="tail",
    )(rims, after, taps_full, gq, gk, gv)


def body(query_feats, key_feats, value_feats, short_taps, long_filter, skip_gain, out_grad):
    tok_rows, width = query_feats.shape
    n_ctx = lax.axis_size("ctx")
    length = tok_rows * n_ctx
    taps_full = widen(short_taps)
    skip = skip_gain.reshape(1, width)
    before = shifted(last_rows(query_feats, key_feats, value_feats), "ctx", 1)
    x, qc, kc, vc = featurize(query_feats, key_feats, value_feats, out_grad, before, taps_full, long_filter.T, n_ctx)
    x = lax.all_to_all(x, "ctx", 0, 0, tiled=True)
    y = longconv(x, 1.0 / math.sqrt(length))
    y = lax.all_to_all(y, "ctx", 0, 0, tiled=True)
    after = shifted(heads(y, qc, kc, vc, out_grad, skip), "ctx", -1)
    mixed_out, gq, gk, gv, rims, gf = spread(y, qc, kc, vc, out_grad, skip, taps_full)
    gq, gk, gv = tail(rims, after, taps_full, gq, gk, gv)
    return (mixed_out, gq, gk, gv, gf.T)


def solution(mesh):
    in_specs = (
        P("ctx", "tp"),
        P("ctx", "tp"),
        P("ctx", "tp"),
        P(None, None, "tp"),
        P("ctx", "tp"),
        P("tp"),
        P("ctx", "tp"),
    )
    out_specs = (P("ctx", "tp"),) * 5
    return jax.shard_map(body, mesh=mesh, in_specs=in_specs, out_specs=out_specs, check_vma=False)
```

```python
import functools
import math

import jax
import jax.numpy as jnp
from jax import lax
from jax.experimental import pallas as pl
from jax.experimental.pallas import tpu as pltpu
from jax.sharding import PartitionSpec as P

D = 8192
SHORT_GROUPS = 512
GROUP = D // SHORT_GROUPS
TAPS = 7
HALO = 8
STRIP = 16
COLS = 256
CHUNK = 64
SPARE = 8
HALVES = 2
LANES = 128
VMEM_LIMIT = 24 * 1024 * 1024

f32 = jnp.float32
bf16 = jnp.bfloat16


def shifted(value, axis, steps):
    count = lax.axis_size(axis)
    initial, last = (max(0, -steps), min(count, count - steps))
    return lax.ppermute(value, axis, [(source, source + steps) for source in range(initial, last)])


def rims_kernel(*refs):
    *ends, last_ref, first_ref = refs
    for which, ref in enumerate(ends[:3]):
        last_ref[which] = ref[...].astype(f32)[HALO:].astype(bf16)
    for which, ref in enumerate(ends[3:]):
        first_ref[which] = ref[...].astype(f32)[:HALO].astype(bf16)


def rims(query, key, value, grad):
    rows, width = query.shape
    end = rows // STRIP - 1
    last = pl.BlockSpec((STRIP, width), lambda i: (end, 0))
    first = pl.BlockSpec((STRIP, width), lambda i: (0, 0))
    return pl.pallas_call(
        rims_kernel,
        grid=(1,),
        in_specs=[last] * 3 + [first] * 4,
        out_specs=[
            pl.BlockSpec((3, HALO, width), lambda i: (0, 0, 0)),
            pl.BlockSpec((4, HALO, width), lambda i: (0, 0, 0)),
        ],
        out_shape=[
            jax.ShapeDtypeStruct((3, HALO, width), bf16),
            jax.ShapeDtypeStruct((4, HALO, width), bf16),
        ],
        compiler_params=pltpu.CompilerParams(vmem_limit_bytes=VMEM_LIMIT),
        name="rims",
    )(*in_hbm(query, key, value, query, key, value, grad))


def widen(short_taps):
    count, _, groups = short_taps.shape
    padded = jnp.pad(short_taps, ((0, 0), (0, HALO - TAPS), (0, 0)))
    return jnp.repeat(padded, GROUP, axis=2).reshape(count * HALO, groups * GROUP)


def tap_rows(taps_ref, which, lanes):
    return [
        jnp.broadcast_to(taps_ref[HALO * which + j : HALO * which + j + 1, lanes], (8, LANES)) for j in range(TAPS)
    ]


def weighted(taps, pieces):
    total = None
    for tap, piece in zip(taps, pieces):
        term = piece.reshape(piece.shape[0] // 8, 8, LANES) * tap[None]
        total = term if total is None else total + term
    return total.reshape(-1, LANES)


def featurize_kernel(
    q_ref, k_ref, v_ref, g_ref, before_ref, taps_ref, f_ref, x_ref, qc_ref, kc_ref, vc_ref, ext, gated, mix
):
    rows, cols = q_ref.shape
    owners = x_ref.shape[0]
    half = cols // owners
    owned_groups = half // GROUP
    start = pl.program_id(0) * cols
    here = pl.ds(pl.multiple_of(start, cols), cols)
    for which, ref in enumerate((q_ref, k_ref, v_ref)):
        ext[which, :HALO, :] = before_ref[which, :, here].astype(f32)
        ext[which, HALO:, :] = ref[...].astype(f32)
    for left in range(0, cols, LANES):
        lanes = slice(left, left + LANES)
        there = pl.ds(pl.multiple_of(start + left, LANES), LANES)
        taps = [tap_rows(taps_ref, which, there) for which in range(3)]
        for lo in range(0, rows, CHUNK):
            part = slice(lo, lo + CHUNK)

            def conv(which):
                first = HALO + lo
                return weighted(taps[which], [ext[which, first - j : first - j + CHUNK, lanes] for j in range(TAPS)])

            key_conv = conv(1)
            kc_ref[part, there] = key_conv
            value_conv = conv(2)
            vc_ref[part, lanes] = value_conv
            gated[part, lanes] = (key_conv * value_conv).astype(bf16)
            query_conv = conv(0)
            qc_ref[part, there] = query_conv
            mix[part, lanes] = (g_ref[part, lanes].astype(f32) * query_conv).astype(bf16)
    for which, signal in enumerate((gated, mix)):
        for part in range(HALVES):
            first = (HALVES * which + part) * half
            piece = signal[LANES * part : LANES * (part + 1), :].T
            x_ref[:, first : first + half, :] = piece.reshape(owners, half, LANES)
    lines = owners * owned_groups
    filt = f_ref[pl.ds(pl.multiple_of(pl.program_id(0) * lines, lines), lines), :].astype(f32)
    blank = jnp.zeros((SPARE - HALVES * owned_groups, LANES), f32)
    for owner in range(owners):
        mine = filt[owner * owned_groups : (owner + 1) * owned_groups]
        pieces = [mine[:, LANES * part : LANES * (part + 1)] for part in range(HALVES)]
        x_ref[owner, 2 * HALVES * half :, :] = jnp.concatenate([*pieces, blank], axis=0).astype(bf16)


def in_hbm(*arrays):
    return [pltpu.with_memory_space_constraint(a, pltpu.HBM) for a in arrays]


def featurize(query, key, value, grad, before, taps_full, filt, n_ctx):
    rows, width = query.shape
    owned = width // n_ctx
    chunk = 2 * HALVES * owned + SPARE
    cols = COLS
    tok = pl.BlockSpec((rows, cols), lambda i: (0, i))
    resident = pl.BlockSpec(memory_space=pltpu.VMEM)
    return pl.pallas_call(
        featurize_kernel,
        grid=(width // cols,),
        in_specs=[
            tok,
            tok,
            tok,
            tok,
            resident,
            resident,
            resident,
        ],
        out_specs=[
            pl.BlockSpec((cols // owned, chunk, LANES), lambda i: (i, 0, 0)),
            resident,
            resident,
            tok,
        ],
        out_shape=[
            pltpu.HBM((n_ctx, chunk, LANES), bf16),
            jax.ShapeDtypeStruct((rows, width), f32),
            jax.ShapeDtypeStruct((rows, width), f32),
            pltpu.HBM((rows, width), f32),
        ],
        scratch_shapes=[
            pltpu.VMEM((3, rows + HALO, cols), f32),
            pltpu.VMEM((rows, cols), bf16),
            pltpu.VMEM((rows, cols), bf16),
        ],
        compiler_params=pltpu.CompilerParams(vmem_limit_bytes=VMEM_LIMIT),
        name="featurize",
    )(*in_hbm(query, key, value, grad), before, taps_full, filt)


WIDE = 2048


def shift_left(value, steps):
    return value if steps == 0 else pltpu.roll(value, value.shape[1] - steps, axis=1)


def build_toeplitz(fpad, which, length, toe):
    toe[:, :LANES] = jnp.zeros((LANES, LANES), bf16)
    for lo in range(0, length, WIDE // 2):
        for p in range(0, LANES, 16):
            lanes = slice(lo + LANES, lo + 2 * LANES + WIDE // 2)
            wide = jnp.broadcast_to(fpad[pl.ds(which, 1), lanes], (16, WIDE // 2 + LANES))
            wide = pltpu.roll(wide, p, axis=1, stride=1, stride_axis=0)
            toe[p : p + 16, lo + LANES : lo + LANES + WIDE // 2] = wide[:, LANES:].astype(bf16)


def longconv_kernel(x_ref, y_hbm, fpad, toe, gpad, zpad, acc, corr, fgrad, ahead, y_ref, sems, *, scale):
    g = pl.program_id(0)
    blocks, chunk, _ = x_ref.shape
    size = HALVES * LANES
    half = (chunk - SPARE) // (2 * HALVES)
    length = blocks * size
    rows = blocks * GROUP
    group = GROUP
    groups = half // group
    batch = 2
    top = batch * group

    @pl.when(g == 0)
    def _():
        fpad[:, : 2 * LANES] = jnp.zeros((SPARE, 2 * LANES), f32)
        for j in range(blocks):
            spare = x_ref[j, 2 * HALVES * half :, :].astype(f32)
            for part in range(HALVES):
                lo = 2 * LANES + size * j + LANES * part
                fpad[:groups, lo : lo + LANES] = spare[groups * part : groups * (part + 1)]
        fgrad[...] = jnp.zeros_like(fgrad)

    build_toeplitz(fpad, g, length, toe)
    gpad[:top, :] = jnp.zeros((top, size), bf16)

    def lines(which, part):
        return pl.ds(pl.multiple_of((HALVES * which + part) * half + g * group, group), group)

    def put(which):
        for part in range(HALVES):
            piece = (acc[:, LANES * part : LANES * (part + 1)] * scale).astype(bf16)
            place = lines(which, part)
            y_ref[:, place, :] = piece.reshape(blocks, group, LANES)
            copy(g, which, part).start()

    def copy(i, which, part):
        place = pl.ds(pl.multiple_of((HALVES * which + part) * half + i * group, group), group)
        return pltpu.make_async_copy(
            y_ref.at[:, place, :], y_hbm.at[:, place, :], sems.at[i, HALVES * which + part]
        )

    for part in range(HALVES):
        lanes = slice(LANES * part, LANES * (part + 1))
        gpad[top:, lanes] = x_ref[:, lines(0, part), :].reshape(rows, LANES)
        zpad[:rows, lanes] = x_ref[:, lines(1, part), :].reshape(rows, LANES)
    zpad[rows:, :] = jnp.zeros((zpad.shape[0] - rows, size), bf16)

    u_t = gpad[top:, :].astype(f32).T.astype(bf16)
    near = rows // 2
    for k in range(blocks):
        depth = rows if k < blocks // 2 else near
        corr[:, size * k : size * (k + 1)] = jnp.dot(
            u_t[:, :depth], zpad[group * k : group * k + depth, :], preferred_element_type=f32
        )
    corr[:, length:] = jnp.zeros((size, corr.shape[1] - length), f32)
    for lo in range(0, length, WIDE):
        total = None
        for p in reversed(range(LANES // 8)):
            part = (
                corr[8 * p : 8 * p + 8, lo : lo + WIDE + LANES]
                + corr[LANES + 8 * p : LANES + 8 * p + 8, lo + LANES : lo + WIDE + 2 * LANES]
            )
            total = part if total is None else shift_left(total, 8) + part
        row = lax.broadcasted_iota(jnp.int32, total.shape, 0)
        for bit in (4, 2, 1):
            total = jnp.where((row & bit) != 0, shift_left(total, bit), total)
        fgrad[pl.ds(g, 1), lo : lo + WIDE] = jnp.sum(total[:, :WIDE], axis=0, keepdims=True) * scale

    def toeplitz_rows(k, width):
        base = 2 * k * LANES
        return jnp.concatenate(
            [toe[:, base + LANES : base + LANES + width], toe[:, base : base + width]], axis=0
        )

    left = jnp.concatenate([gpad[top - group * i : top - group * i + rows, :] for i in range(batch)], axis=1)
    for kb in range(blocks // batch):
        first = top * kb
        right = jnp.concatenate([toeplitz_rows(batch * kb + i, size) for i in range(batch)], axis=0)
        part = jnp.dot(left[: rows - first], right, preferred_element_type=f32)
        acc[first:, :] = part if kb == 0 else acc[first:, :] + part
    put(0)

    for kb in range(blocks // batch):
        first = top * kb
        right = toeplitz_rows(batch * kb, batch * size)
        count = rows - first
        left = jnp.concatenate(
            [zpad[first + group * i : first + group * i + count, :] for i in range(batch)], axis=1
        )
        part = lax.dot_general(left, right, (((1,), (1,)), ((), ())), preferred_element_type=f32)
        acc[:count, :] = part if kb == 0 else acc[:count, :] + part
    put(1)

    @pl.when(g == groups - 1)
    def _():
        bits = group.bit_length() - 1
        token = lax.broadcasted_iota(jnp.int32, (LANES, LANES), 0)
        lane = lax.broadcasted_iota(jnp.int32, (LANES, LANES), 1)
        spot = ((lane >> bits) == HALO - 1 - token).astype(f32).astype(bf16)
        channel = lax.broadcasted_iota(jnp.int32, (group, LANES), 0)
        own = (lax.broadcasted_iota(jnp.int32, (group, LANES), 1) & (group - 1)) == channel
        block = lax.broadcasted_iota(jnp.int32, (blocks, rows), 1) >> bits
        after = (block == lax.broadcasted_iota(jnp.int32, (blocks, rows), 0) + 1).astype(f32).astype(bf16)
        for which in range(2):
            for i in range(groups):
                first = HALVES * which * half + i * group
                piece = y_ref[:, first : first + group, :].reshape(rows, LANES)
                tall = jnp.dot(piece, spot, preferred_element_type=f32).reshape(blocks, group, LANES)
                tall = jnp.where(own[None], tall, 0.0).reshape(rows, LANES).astype(bf16)
                place = (which * groups + i) * blocks
                ahead[place : place + blocks, :] = jnp.dot(after, tall, preferred_element_type=f32)
        for j in range(blocks):
            starts = [size * j + LANES * part for part in range(HALVES)]
            pieces = [fgrad[:groups, lo : lo + LANES] for lo in starts]
            pieces += [ahead[blocks * i + j : blocks * i + j + 1, :] for i in range(2 * groups)]
            y_ref[j, 2 * HALVES * half :, :] = jnp.concatenate(pieces, axis=0).astype(bf16)
        spare = pl.ds(2 * HALVES * half, SPARE)
        spare_out = pltpu.make_async_copy(
            y_ref.at[:, spare, :], y_hbm.at[:, spare, :], sems.at[0, 2 * HALVES]
        )
        spare_out.start()
        for i in range(groups):
            for which in range(2):
                for part in range(HALVES):
                    copy(i, which, part).wait()
        spare_out.wait()


def longconv(x, scale):
    blocks, chunk, _ = x.shape
    size = HALVES * LANES
    length = blocks * size
    rows = blocks * GROUP
    groups = (chunk - SPARE) // (2 * HALVES) // GROUP
    return pl.pallas_call(
        functools.partial(longconv_kernel, scale=scale),
        grid=(groups,),
        in_specs=[pl.BlockSpec(memory_space=pltpu.VMEM)],
        out_specs=pl.BlockSpec(memory_space=pltpu.HBM),
        out_shape=pltpu.HBM(x.shape, bf16),
        scratch_shapes=[
            pltpu.VMEM((SPARE, length + 2 * LANES), f32),
            pltpu.VMEM((LANES, length + LANES), bf16),
            pltpu.VMEM((rows + 2 * GROUP, size), bf16),
            pltpu.VMEM((rows + rows // 2, size), bf16),
            pltpu.VMEM((rows, size), f32),
            pltpu.VMEM((size, length + 2 * LANES), f32),
            pltpu.VMEM((SPARE, length), f32),
            pltpu.VMEM((2 * groups * blocks, LANES), f32),
            pltpu.VMEM(x.shape, bf16),
            pltpu.SemaphoreType.DMA((groups, 2 * HALVES + 1)),
        ],
        compiler_params=pltpu.CompilerParams(vmem_limit_bytes=VMEM_LIMIT),
        name="longconv",
    )(x)


def tokens(y_ref, block, count):
    owners = y_ref.shape[0]
    return y_ref[:, block * count : (block + 1) * count, :].reshape(owners * count, LANES).T


def grads(conv, back, qc, kc, vc, grad, skip):
    gated = (kc * vc).astype(bf16).astype(f32)
    grad_mix = (grad * qc).astype(bf16).astype(f32)
    mixed = conv + skip * gated
    grad_gate = back + skip * grad_mix
    return mixed, grad * mixed, grad_gate * vc, grad_gate * kc


def unpacked(lines):
    shape = (HALO, LANES)
    lane = lax.broadcasted_iota(jnp.int32, shape, 1)
    token = lax.broadcasted_iota(jnp.int32, shape, 0)
    total = jnp.zeros(shape, f32)
    for r, line in enumerate(lines):
        base = GROUP * ((r + 1) % HALO)
        moved = jnp.broadcast_to(line, shape)
        moved = pltpu.roll(moved, base, axis=1) if base else moved
        for bit in (1, 2, 4):
            moved = jnp.where((token & bit) != 0, pltpu.roll(moved, GROUP * bit, axis=1), moved)
        total = jnp.where(lane // GROUP == r, moved, total)
    return total


def spread_kernel(
    y_ref, qc_ref, kc_ref, vc_ref, g_ref, skip_ref, taps_ref, last_ref, next_ref,
    out_ref, gq_ref, gk_ref, gv_ref, gf_ref, conv, back, ext, edge,
):
    rows, cols = g_ref.shape
    half = (y_ref.shape[1] - SPARE) // (2 * HALVES)
    owners = cols // half
    owned_groups = gf_ref.shape[0] // owners
    step = pl.program_id(0)
    y_ref = y_ref.at[pl.ds(step * owners, owners)]
    lines, ends = [], []
    for owner in range(owners):
        spare = y_ref[owner, 2 * HALVES * half :, :].astype(f32)
        pieces = [spare[owned_groups * part : owned_groups * (part + 1)] for part in range(HALVES)]
        lines.append(jnp.concatenate(pieces, axis=1))
        ends.append(spare[HALVES * owned_groups :])
    gf_ref[...] = jnp.concatenate(lines, axis=0).astype(bf16)
    for part in range(HALVES):
        conv[LANES * part : LANES * (part + 1), :] = tokens(y_ref, part, half)
        back[LANES * part : LANES * (part + 1), :] = tokens(y_ref, HALVES + part, half)
    for left in range(0, cols, LANES):
        lanes = slice(left, left + LANES)
        there = pl.ds(pl.multiple_of(step * cols + left, LANES), LANES)
        taps = [tap_rows(taps_ref, which, there) for which in range(3)]
        after = []
        for which in range(3):
            edge[which, :HALO, :] = last_ref[which, :, there].astype(f32)
            edge[which, HALO:, :] = next_ref[which, :, there].astype(f32)
            after.append(weighted(taps[which], [edge[which, HALO - j : 2 * HALO - j, :] for j in range(TAPS)]))
        first = left // GROUP
        tile = [divmod(first + r, owned_groups) for r in range(LANES // GROUP)]
        conv_next, back_next = [
            unpacked([ends[o][owned_groups * kind + i : owned_groups * kind + i + 1] for o, i in tile])
            for kind in range(2)
        ]
        _, *signals = grads(conv_next, back_next, *after, next_ref[3, :, there].astype(f32), skip_ref[:, there])
        for which in range(3):
            ext[which, rows:, lanes] = signals[which]
        for lo in reversed(range(0, rows, CHUNK)):
            part = slice(lo, lo + CHUNK)
            qc = qc_ref[part, there]
            mixed, *signals = grads(
                conv[part, lanes].astype(f32),
                back[part, lanes].astype(f32),
                qc,
                kc_ref[part, there],
                vc_ref[part, lanes],
                g_ref[part, lanes].astype(f32),
                skip_ref[:, there],
            )
            out_ref[part, lanes] = (qc * mixed).astype(bf16)
            for which, target in enumerate((gq_ref, gk_ref, gv_ref)):
                ext[which, part, lanes] = signals[which]
                pieces = [ext[which, lo + j : lo + j + CHUNK, lanes] for j in range(TAPS)]
                target[part, lanes] = weighted(taps[which], pieces).astype(bf16)


def spread(y, qc, kc, vc, grad, skip, taps_full, last, following):
    rows, width = qc.shape
    cols = COLS
    tok = pl.BlockSpec((rows, cols), lambda i: (0, i))
    resident = pl.BlockSpec(memory_space=pltpu.VMEM)
    return pl.pallas_call(
        spread_kernel,
        grid=(width // cols,),
        in_specs=[resident] * 3 + [tok] * 2 + [resident] * 4,
        out_specs=[tok] * 4
        + [
            pl.BlockSpec((cols // GROUP, rows), lambda i: (i, 0)),
        ],
        out_shape=[jax.ShapeDtypeStruct((rows, width), bf16)] * 4
        + [jax.ShapeDtypeStruct((width // GROUP, rows), bf16)],
        scratch_shapes=[
            pltpu.VMEM((rows, cols), bf16),
            pltpu.VMEM((rows, cols), bf16),
            pltpu.VMEM((3, rows + HALO, cols), f32),
            pltpu.VMEM((3, 2 * HALO, LANES), f32),
        ],
        compiler_params=pltpu.CompilerParams(vmem_limit_bytes=VMEM_LIMIT),
        cost_estimate=pl.CostEstimate(flops=12_000_000, bytes_accessed=8_000_000, transcendentals=0),
        name="spread",
    )(y, qc, kc, vc, *in_hbm(grad), skip, taps_full, last, following)


def body(query_feats, key_feats, value_feats, short_taps, long_filter, skip_gain, out_grad):
    tok_rows, width = query_feats.shape
    n_ctx = lax.axis_size("ctx")
    length = tok_rows * n_ctx
    taps_full = widen(short_taps)
    skip = skip_gain.reshape(1, width)
    last, first = rims(query_feats, key_feats, value_feats, out_grad)
    before = shifted(last, "ctx", 1)
    following = shifted(first, "ctx", -1)
    x, qc, kc, vc = featurize(query_feats, key_feats, value_feats, out_grad, before, taps_full, long_filter.T, n_ctx)
    x = lax.all_to_all(x, "ctx", 0, 0, tiled=True)
    y = longconv(x, 1.0 / math.sqrt(length))
    y = lax.all_to_all(y, "ctx", 0, 0, tiled=True)
    mixed_out, gq, gk, gv, gf = spread(y, qc, kc, vc, out_grad, skip, taps_full, last, following)
    return (mixed_out, gq, gk, gv, gf.T)


def solution(mesh):
    in_specs = (
        P("ctx", "tp"),
        P("ctx", "tp"),
        P("ctx", "tp"),
        P(None, None, "tp"),
        P("ctx", "tp"),
        P("tp"),
        P("ctx", "tp"),
    )
    out_specs = (P("ctx", "tp"),) * 5
    return jax.shard_map(body, mesh=mesh, in_specs=in_specs, out_specs=out_specs, check_vma=False)
```
